32 devices in a mesh: ens: 2 (over y), rows: 8 (over z, x), fa: 2 (over core).
Axes of the slice: x: 2, y: 2, z: 4, core: 2. Of those that a mesh axis runs over, the one named last changes fastest.
Arguments:
- init_fields: float32 [2, 16, 128, 1792], P('fa', 'ens', 'rows'), parts along dimension 1, may hold values from -6 to 6
- streamwise: float32 [128, 1792], P('rows'), may hold values from 0 to 0.25
- crossflow: float32 [128, 1792], P('rows'), may hold values from -0.15 to 0.15
- diffusivity: float32 [128, 1792], P('rows'), may hold values from 0.1 to 0.24
- obstacle: int32 [128, 1792], P('rows'), may hold values from 0 to 1, as said below
- cell_weight: float32 [128, 1792], P('rows'), may hold values from 1 to 30, as said below
Outputs:
- final_fields: float32 [2, 16, 128, 1792], P('fa', 'ens', 'rows'), parts along dimension 1
- hankel: float32 [64, 32], P('ens'), parts along dimension 0
The draws below stay inside these ranges and needn't reach their ends.
There are 2 independent parts, one for each index of `ens`. The reference program is written for one: setup_inputs(seed, part) draws one part's arguments, and reference() takes and returns one part's arrays. A program takes and returns all parts, laid end to end along the dimension named above; an argument that names none is the same for every part. Nothing has to cross between parts.
Inputs may be any that keep to these rules, and one draw needn't show every extreme that they name: `obstacle`: 1 on the cells of one disk, 0 elsewhere. `cell_weight`: positive areas.
All inputs are finite; a program needn't handle non-finite values.
Results may differ from the reference program's by a relative error of at most 0.0018.
Values may be sent and summed in bfloat16 or wider, within the bound.
No kernel may reach another device: no remote copies, remote signals or barrier semaphores. Data moves between devices by JAX's collectives and lax.ppermute only.
A program may use at most 64 MiB of HBM per device.

```python
import math
import jax
import jax.numpy as jnp

ROWS_DEV = 16
COLS = 1792
INPUTS = 8
NSNAP = 4
STRIDE = 3
NR = 128
SNAPS = 32


def draw_obstacle(key, part):
    subkeys = jax.random.split(key, 3)
    center_row = jax.random.randint(subkeys[0], (), NR // 4, 3 * NR // 4)
    center_col = jax.random.randint(subkeys[1], (), COLS // 8, COLS // 4 + 1)
    radius = jax.random.randint(subkeys[2], (), 2, ROWS_DEV + 1)
    row_gap = jnp.arange(NR, dtype=jnp.int32)[:, None] - center_row
    col_gap = jnp.arange(COLS, dtype=jnp.int32)[None, :] - center_col
    return (row_gap * row_gap + col_gap * col_gap <= radius * radius).astype(jnp.int32)


def draw_cell_weight(key, part):
    row_level = jnp.arange(NR, dtype=jnp.float32)[:, None] / NR
    rising = jnp.exp(math.log(3.0) * row_level)
    spread = jnp.exp(jax.random.uniform(key, (NR, COLS), jnp.float32, 0.0, math.log(10.0)))
    return (rising * spread).astype(jnp.float32)


def levels(key, shape, pieces, least, largest):
    def one(axis_at, shards_of):
        steps = jax.random.uniform(jax.random.fold_in(jax.random.fold_in(key, 6), axis_at), (shards_of,), jnp.float32, least / len(pieces), largest / len(pieces))
        return jnp.repeat(jnp.exp(steps), shape[axis_at] // shards_of).reshape((-1,) + (1,) * (len(shape) - axis_at - 1))

    loudness = one(*pieces[0])
    for cut in pieces[1:]:
        loudness = loudness * one(*cut)
    return loudness


def bell_draw(rng, shape, scale, limit, pieces=(), held_as=jnp.bfloat16):
    array = scale * jax.random.normal(rng, shape, jnp.float32)
    if pieces:
        array = array * levels(rng, shape, pieces, -0.22, 0.18)
    return jnp.clip(array, -limit, limit).astype(held_as)


def setup_inputs(seed: int = 0, part: int = 0) -> dict:
    keys = jax.random.split(jax.random.key(seed), 7)
    own_keys = jax.random.split(jax.random.fold_in(keys[6], part), 7)
    return {
        "init_fields": bell_draw(own_keys[0], (2, INPUTS, NR, COLS), 1.0, 6.0, ((0, 2), (2, 8)), jnp.float32),
        "streamwise": jnp.clip(0.25 * jax.random.uniform(keys[1], (NR, COLS), jnp.float32) ** levels(keys[1], (NR, COLS), ((0, 8),), -0.2, 0.2), 0.0, 0.25),
        "crossflow": jnp.clip(jax.random.uniform(keys[2], (NR, COLS), jnp.float32, -0.15, 0.15) * levels(keys[2], (NR, COLS), ((0, 8),), -0.4, 0.0), -0.15, 0.15),
        "diffusivity": jnp.clip(jnp.exp(math.log(0.24) - 0.8754687 * jax.random.uniform(keys[3], (NR, COLS), jnp.float32) ** levels(keys[3], (NR, COLS), ((0, 8),), -0.2, 0.2)), 0.1, 0.24),
        "obstacle": draw_obstacle(jax.random.fold_in(keys[6], 71), part),
        "cell_weight": draw_cell_weight(jax.random.fold_in(keys[6], 71), part),
    }


def shifted(source, row_shift, col_shift):
    row_count, col_count = source.shape
    padded = jnp.pad(source, 1)
    return padded[1 + row_shift:1 + row_shift + row_count, 1 + col_shift:1 + col_shift + col_count]

def advance(current, weights, before, after_mask):
    east_weight, west_weight, north_weight, south_weight, centre_weight = weights
    masked = before * current
    widened = jnp.pad(masked, ((0, 0), (1, 1), (1, 1)))
    summed = masked + east_weight * widened[:, 1:-1, 2:] + west_weight * widened[:, 1:-1, :-2]
    summed = summed + north_weight * widened[:, 2:, 1:-1] + south_weight * widened[:, :-2, 1:-1]
    summed = summed + centre_weight * masked
    return after_mask * summed

def run_system(current, weights, before, after_mask, scaling):
    kept_parts = []
    for snap_index in range(NSNAP):
        for inner_step in range(STRIDE):
            current = advance(current, weights, before, after_mask)
        kept_parts.append((scaling * current).astype(jnp.bfloat16))
    return (current, jnp.stack(kept_parts))

def reference(init_fields, streamwise, crossflow, diffusivity, obstacle, cell_weight):
    solid_cells = obstacle.astype(jnp.float32)
    open_cells = 1.0 - solid_cells
    centre_weight = -4.0 * diffusivity
    forward = (-streamwise / 2 + diffusivity, streamwise / 2 + diffusivity, -crossflow / 2 + diffusivity, crossflow / 2 + diffusivity, centre_weight)
    adjoint = (shifted(streamwise, 0, 1) / 2 + shifted(diffusivity, 0, 1), -shifted(streamwise, 0, -1) / 2 + shifted(diffusivity, 0, -1), shifted(crossflow, 1, 0) / 2 + shifted(diffusivity, 1, 0), -shifted(crossflow, -1, 0) / 2 + shifted(diffusivity, -1, 0), centre_weight)
    direct_final, direct_snaps = run_system(init_fields[0], forward, 1.0, open_cells, 1.0)
    adjoint_final, adjoint_snaps = run_system(init_fields[1], adjoint, open_cells, 1.0, cell_weight)
    product = jnp.dot(adjoint_snaps.reshape(SNAPS, -1), direct_snaps.reshape(SNAPS, -1).T, preferred_element_type=jnp.float32)
    hankel = product * (1.0 / math.sqrt(NR * COLS))
    return (jnp.stack([direct_final, adjoint_final]), hankel)
```

```python
import functools
import math

import jax
import jax.numpy as jnp
from jax import lax
from jax.experimental import pallas as pl
from jax.experimental.pallas import tpu as pltpu
from jax.sharding import PartitionSpec as P

NSNAP = 4
STRIDE = 3
HALO = NSNAP * STRIDE
LANES = 128
SUB = 8


def up8(count):
    return -(-count // SUB) * SUB


def tiled(array):
    inputs, rows, cols = array.shape
    split = array.reshape(inputs, rows // SUB, SUB, cols // LANES, LANES)
    return split.transpose(0, 1, 3, 2, 4).reshape(-1, LANES)


def untiled(array, shape):
    inputs, rows, cols = shape
    split = array.reshape(inputs, rows // SUB, cols // LANES, SUB, LANES)
    return split.transpose(0, 1, 3, 2, 4).reshape(shape)


def tile_of(rows, cols, row, tile, inputs):
    start = (row // SUB * (cols // LANES) + tile) * SUB + row % SUB
    return pl.ds(start, inputs, stride=rows * cols // LANES)


def pack_kernel(rows, inputs, field, along, across, viscous, solid, up, down, coefs):
    cols = along.shape[1]
    signed = jnp.where(solid[...] != 0, -viscous[...], viscous[...])
    for out, first in ((up, rows - HALO), (down, 0)):
        for step in range(HALO):
            for tile in range(cols // LANES):
                part = field[tile_of(rows, cols, first + step, tile, inputs), :]
                at = (slice(step * inputs, (step + 1) * inputs), slice(tile * LANES, (tile + 1) * LANES))
                out[at] = part.astype(out.dtype)
        coefs[0:HALO, :] = along[first : first + HALO, :]
        coefs[HALO : 2 * HALO, :] = across[first : first + HALO, :]
        coefs[2 * HALO : 3 * HALO, :] = signed[first : first + HALO]
        out[HALO * inputs :, :] = coefs[...].astype(out.dtype)


def march_kernel(
    rows, inputs, adjoint_ref, field, along, across, viscous, solid, area, low, high,
    final, kept, sent,
    state, coefs, raw_x, raw_y, raw_d, east_w, west_w, north_w, south_w, centre_w, scale_w,
):
    adjoint = adjoint_ref[0]
    is_adjoint = adjoint == 1
    cols = along.shape[1]
    half = cols // 2
    span = rows + 2 * HALO
    tiles = cols // LANES

    raw_x[HALO : HALO + rows, :] = along[...]
    raw_y[HALO : HALO + rows, :] = across[...]
    raw_d[HALO : HALO + rows, :] = jnp.where(solid[...] != 0, -viscous[...], viscous[...])
    for source, first in ((low, 0), (high, HALO + rows)):
        coefs[...] = source[HALO * inputs :, :].astype(jnp.float32)
        raw_x[first : first + HALO, :] = coefs[0:HALO, :]
        raw_y[first : first + HALO, :] = coefs[HALO : 2 * HALO, :]
        raw_d[first : first + HALO, :] = coefs[2 * HALO : 3 * HALO, :]
    column = lax.broadcasted_iota(jnp.int32, (SUB, cols), 1)
    for first in range(0, span, SUB):
        at = slice(first, first + SUB)
        signed = raw_d[at, :]
        opened = jnp.where(signed < 0, 0.0, 1.0)
        spread = jnp.abs(signed)
        half_x = raw_x[at, :] * 0.5
        half_y = raw_y[at, :] * 0.5
        east = opened * (spread - half_x)
        west = opened * (spread + half_x)
        north = opened * (spread - half_y)
        south = opened * (spread + half_y)
        east_a = pltpu.roll(west, cols - 1, 1)
        west_a = pltpu.roll(east, 1, 1)
        for ref, values in (
            (east_w, jnp.where(column == cols - 1, 0.0, jnp.where(is_adjoint, east_a, east))),
            (west_w, jnp.where(column == 0, 0.0, jnp.where(is_adjoint, west_a, west))),
            (north_w, jnp.where(is_adjoint, south, north)),
            (south_w, jnp.where(is_adjoint, north, south)),
            (centre_w, opened * (1.0 - 4.0 * spread)),
        ):
            for tile in range(tiles):
                ref[tile * span + first : tile * span + first + SUB, :] = values[
                    :, tile * LANES : (tile + 1) * LANES
                ]
    scale = jnp.where(is_adjoint, area[...], 1.0)
    for tile in range(tiles):
        scale_w[tile * rows : (tile + 1) * rows, :] = scale[:, tile * LANES : (tile + 1) * LANES]

    state[0, 0 : HALO * inputs, :] = low[0 : HALO * inputs, :].astype(jnp.float32)
    state[0, (HALO + rows) * inputs :, :] = high[0 : HALO * inputs, :].astype(jnp.float32)
    for row in range(rows):
        for tile in range(tiles):
            at = (slice((HALO + row) * inputs, (HALO + row + 1) * inputs), slice(tile * LANES, (tile + 1) * LANES))
            state[(0, *at)] = field[tile_of(rows, cols, row, tile, inputs), :]

    lane = lax.broadcasted_iota(jnp.int32, (inputs, LANES), 1)
    group = 2

    for step in range(1, HALO + 1):
        src, dst = (step - 1) % 2, step % 2

        def advance(index, carry, step=step, src=src, dst=dst):
            row0 = step + index * group

            def cell(row, tile):
                at = pl.ds(pl.multiple_of(row * inputs, inputs), inputs)
                return state[src, at, tile * LANES : (tile + 1) * LANES]

            def weight(ref, row, tile):
                return ref[pl.ds(tile * span + row, inputs, stride=0), :]

            for tile in range(tiles):
                column = [cell(row0 + n - 1, tile) for n in range(group + 2)]
                for n in range(group):
                    row = row0 + n
                    here = column[n + 1]
                    after = cell(row, (tile + 1) % tiles)
                    before = cell(row, (tile - 1) % tiles)
                    eastern = pltpu.roll(jnp.where(lane == 0, after, here), LANES - 1, 1)
                    western = pltpu.roll(jnp.where(lane == LANES - 1, before, here), 1, 1)
                    total = weight(centre_w, row, tile) * here
                    total += weight(east_w, row, tile) * eastern
                    total += weight(west_w, row, tile) * western
                    total += weight(north_w, row + adjoint, tile) * column[n + 2]
                    total += weight(south_w, row - adjoint, tile) * column[n]
                    at = pl.ds(pl.multiple_of(row * inputs, inputs), inputs)
                    state[dst, at, tile * LANES : (tile + 1) * LANES] = total
            return carry

        lax.fori_loop(0, (span - 2 * step) // group, advance, 0)
        if step % STRIDE == 0:
            snap = slice((step // STRIDE - 1) * inputs, (step // STRIDE) * inputs)

            def record(row, carry, dst=dst, snap=snap):
                at = pl.ds(pl.multiple_of((HALO + row) * inputs, inputs), inputs)
                for out, first in ((kept, adjoint * (tiles // 2)), (sent, (1 - adjoint) * (tiles // 2))):
                    for tile in range(tiles // 2):
                        where = pl.ds(pl.multiple_of((first + tile) * LANES, LANES), LANES)
                        factor = scale_w[pl.ds((first + tile) * rows + row, inputs, stride=0), :]
                        value = state[dst, at, where] * factor
                        out_at = pl.ds(pl.multiple_of(row * half + tile * LANES, LANES), LANES)
                        out[snap, out_at] = value.astype(out.dtype)
                return carry

            lax.fori_loop(0, rows, record, 0)
    for row in range(rows):
        for tile in range(tiles):
            at = (slice((HALO + row) * inputs, (HALO + row + 1) * inputs), slice(tile * LANES, (tile + 1) * LANES))
            final[tile_of(rows, cols, row, tile, inputs), :] = state[(HALO % 2, *at)]


def local(init_fields, streamwise, crossflow, diffusivity, obstacle, cell_weight):
    adjoint = lax.axis_index("fa").astype(jnp.int32)
    _, inputs, rows, cols = init_fields.shape
    field = tiled(init_fields[0])
    coef_rows = up8(3 * HALO)
    packed_rows = HALO * inputs + coef_rows
    span = rows + 2 * HALO
    half = cols // 2
    vmem = pl.BlockSpec(memory_space=pltpu.VMEM)
    bf16, f32 = jnp.bfloat16, jnp.float32

    packed = jax.ShapeDtypeStruct((packed_rows, cols), bf16)
    up, down = pl.pallas_call(
        functools.partial(pack_kernel, rows, inputs),
        out_shape=(packed, packed),
        in_specs=[vmem] * 5,
        out_specs=(vmem, vmem),
        scratch_shapes=[pltpu.VMEM((coef_rows, cols), f32)],
        name="pack",
    )(field, streamwise, crossflow, diffusivity, obstacle)
    size = lax.axis_size("rows")
    low = lax.ppermute(up, "rows", [(i, i + 1) for i in range(size - 1)])
    high = lax.ppermute(down, "rows", [(i + 1, i) for i in range(size - 1)])

    snaps = jax.ShapeDtypeStruct((NSNAP * inputs, rows * half), bf16)
    grid_rows = pltpu.VMEM((span, cols), f32)
    weights = pltpu.VMEM((cols // LANES * span, LANES), f32)
    final, kept, sent = pl.pallas_call(
        functools.partial(march_kernel, rows, inputs),
        out_shape=(jax.ShapeDtypeStruct(field.shape, f32), snaps, snaps),
        in_specs=[pl.BlockSpec(memory_space=pltpu.SMEM)] + [vmem] * 8,
        out_specs=(vmem,) * 3,
        scratch_shapes=[
            pltpu.VMEM((2, span * inputs, cols), f32),
            pltpu.VMEM((coef_rows, cols), f32),
            *[grid_rows] * 3,
            *[weights] * 5,
            pltpu.VMEM((cols // LANES * rows, LANES), f32),
        ],
        name="march",
    )(adjoint[None], field, streamwise, crossflow, diffusivity, obstacle, cell_weight, low, high)

    other = lax.ppermute(sent, "fa", [(0, 1), (1, 0)])
    product = lax.dot_general(kept, other, (((1,), (1,)), ((), ())), preferred_element_type=f32)
    total = jnp.where(adjoint == 1, product, product.T)
    total = total + lax.ppermute(total, "fa", [(0, 1), (1, 0)])
    if size & (size - 1) == 0:
        stride = 1
        while stride < size:
            total = total + lax.ppermute(total, "rows", [(i, i ^ stride) for i in range(size)])
            stride *= 2
    else:
        total = lax.psum(total, "rows")
    hankel = total * (1.0 / math.sqrt(rows * size * cols))
    return (untiled(final, init_fields.shape[1:])[None], hankel)


def solution(mesh):
    placed = (
        P("fa", "ens", "rows", None),
        P("rows", None),
        P("rows", None),
        P("rows", None),
        P("rows", None),
        P("rows", None),
    )
    return jax.shard_map(
        local,
        mesh=mesh,
        in_specs=placed,
        out_specs=(P("fa", "ens", "rows", None), P("ens", None)),
        check_vma=False,
    )
```

```python
import functools
import math

import jax
import jax.numpy as jnp
from jax import lax
from jax.experimental import pallas as pl
from jax.experimental.pallas import tpu as pltpu
from jax.sharding import PartitionSpec as P

NSNAP = 4
STRIDE = 3
HALO = NSNAP * STRIDE
LANES = 128
SUB = 8


def up8(count):
    return -(-count // SUB) * SUB


def tiled(array):
    inputs, rows, cols = array.shape
    split = array.reshape(inputs, rows // SUB, SUB, cols // LANES, LANES)
    return split.transpose(0, 1, 3, 2, 4).reshape(-1, LANES)


def untiled(array, shape):
    inputs, rows, cols = shape
    split = array.reshape(inputs, rows // SUB, cols // LANES, SUB, LANES)
    return split.transpose(0, 1, 3, 2, 4).reshape(shape)


def tile_of(rows, cols, row, tile, inputs):
    start = (row // SUB * (cols // LANES) + tile) * SUB + row % SUB
    return pl.ds(start, inputs, stride=rows * cols // LANES)


def pack_kernel(rows, inputs, field, along, across, viscous, solid, up, down, coefs):
    cols = along.shape[1]
    signed = jnp.where(solid[...] != 0, -viscous[...], viscous[...])
    for out, first in ((up, rows - HALO), (down, 0)):
        for step in range(HALO):
            for tile in range(cols // LANES):
                part = field[tile_of(rows, cols, first + step, tile, inputs), :]
                at = (slice(step * inputs, (step + 1) * inputs), slice(tile * LANES, (tile + 1) * LANES))
                out[at] = part.astype(out.dtype)
        coefs[0:HALO, :] = along[first : first + HALO, :]
        coefs[HALO : 2 * HALO, :] = across[first : first + HALO, :]
        coefs[2 * HALO : 3 * HALO, :] = signed[first : first + HALO]
        out[HALO * inputs :, :] = coefs[...].astype(out.dtype)


def march_kernel(
    rows, inputs, adjoint_ref, field, along, across, viscous, solid, area, low, high,
    final, kept, sent,
    state_a, state_b, coefs, raw_x, raw_y, raw_d, east_w, west_w, north_w, south_w, centre_w, scale_w,
):
    adjoint = adjoint_ref[0]
    is_adjoint = adjoint == 1
    cols = along.shape[1]
    half = cols // 2
    span = rows + 2 * HALO
    tiles = cols // LANES

    raw_x[HALO : HALO + rows, :] = along[...]
    raw_y[HALO : HALO + rows, :] = across[...]
    raw_d[HALO : HALO + rows, :] = jnp.where(solid[...] != 0, -viscous[...], viscous[...])
    for source, first in ((low, 0), (high, HALO + rows)):
        coefs[...] = source[HALO * inputs :, :].astype(jnp.float32)
        raw_x[first : first + HALO, :] = coefs[0:HALO, :]
        raw_y[first : first + HALO, :] = coefs[HALO : 2 * HALO, :]
        raw_d[first : first + HALO, :] = coefs[2 * HALO : 3 * HALO, :]
    column = lax.broadcasted_iota(jnp.int32, (SUB, cols), 1)
    for first in range(0, span, SUB):
        at = slice(first, first + SUB)
        signed = raw_d[at, :]
        opened = jnp.where(signed < 0, 0.0, 1.0)
        spread = jnp.abs(signed)
        half_x = raw_x[at, :] * 0.5
        half_y = raw_y[at, :] * 0.5
        east = opened * (spread - half_x)
        west = opened * (spread + half_x)
        north = opened * (spread - half_y)
        south = opened * (spread + half_y)
        east_a = pltpu.roll(west, cols - 1, 1)
        west_a = pltpu.roll(east, 1, 1)
        for ref, values in (
            (east_w, jnp.where(column == cols - 1, 0.0, jnp.where(is_adjoint, east_a, east))),
            (west_w, jnp.where(column == 0, 0.0, jnp.where(is_adjoint, west_a, west))),
            (north_w, jnp.where(is_adjoint, south, north)),
            (south_w, jnp.where(is_adjoint, north, south)),
            (centre_w, opened * (1.0 - 4.0 * spread)),
        ):
            for tile in range(tiles):
                ref[tile * span + first : tile * span + first + SUB, :] = values[
                    :, tile * LANES : (tile + 1) * LANES
                ]
    scale = jnp.where(is_adjoint, area[...], 1.0)
    for tile in range(tiles):
        scale_w[tile * rows : (tile + 1) * rows, :] = scale[:, tile * LANES : (tile + 1) * LANES]

    state_a[0 : HALO * inputs, :] = low[0 : HALO * inputs, :].astype(jnp.float32)
    state_a[(HALO + rows) * inputs :, :] = high[0 : HALO * inputs, :].astype(jnp.float32)
    for row in range(rows):
        for tile in range(tiles):
            at = (slice((HALO + row) * inputs, (HALO + row + 1) * inputs), slice(tile * LANES, (tile + 1) * LANES))
            state_a[at] = field[tile_of(rows, cols, row, tile, inputs), :]

    states = (state_a, state_b)
    lane = lax.broadcasted_iota(jnp.int32, (inputs, LANES), 1)
    group = 2

    for step in range(1, HALO + 1):
        src, dst = states[(step - 1) % 2], states[step % 2]

        def advance(index, carry, step=step, src=src, dst=dst):
            row0 = step + index * group

            def cell(row, tile):
                at = pl.ds(pl.multiple_of(row * inputs, inputs), inputs)
                return src[at, tile * LANES : (tile + 1) * LANES]

            def weight(ref, row, tile):
                return ref[pl.ds(tile * span + row, inputs, stride=0), :]

            for tile in range(tiles):
                column = [cell(row0 + n - 1, tile) for n in range(group + 2)]
                for n in range(group):
                    row = row0 + n
                    here = column[n + 1]
                    after = cell(row, (tile + 1) % tiles)
                    before = cell(row, (tile - 1) % tiles)
                    eastern = pltpu.roll(jnp.where(lane == 0, after, here), LANES - 1, 1)
                    western = pltpu.roll(jnp.where(lane == LANES - 1, before, here), 1, 1)
                    total = weight(centre_w, row, tile) * here
                    total += weight(east_w, row, tile) * eastern
                    total += weight(west_w, row, tile) * western
                    total += weight(north_w, row + adjoint, tile) * column[n + 2]
                    total += weight(south_w, row - adjoint, tile) * column[n]
                    at = pl.ds(pl.multiple_of(row * inputs, inputs), inputs)
                    dst[at, tile * LANES : (tile + 1) * LANES] = total
            return carry

        lax.fori_loop(0, (span - 2 * step) // group, advance, 0)
        if step % STRIDE == 0:
            snap = slice((step // STRIDE - 1) * inputs, (step // STRIDE) * inputs)

            def record(row, carry, dst=dst, snap=snap):
                at = pl.ds(pl.multiple_of((HALO + row) * inputs, inputs), inputs)
                for out, first in ((kept, adjoint * (tiles // 2)), (sent, (1 - adjoint) * (tiles // 2))):
                    for tile in range(tiles // 2):
                        where = pl.ds(pl.multiple_of((first + tile) * LANES, LANES), LANES)
                        factor = scale_w[pl.ds((first + tile) * rows + row, inputs, stride=0), :]
                        value = dst[at, where] * factor
                        out_at = pl.ds(pl.multiple_of(row * half + tile * LANES, LANES), LANES)
                        out[snap, out_at] = value.astype(out.dtype)
                return carry

            lax.fori_loop(0, rows, record, 0)
    for row in range(rows):
        for tile in range(tiles):
            at = (slice((HALO + row) * inputs, (HALO + row + 1) * inputs), slice(tile * LANES, (tile + 1) * LANES))
            final[tile_of(rows, cols, row, tile, inputs), :] = states[HALO % 2][at]


def local(init_fields, streamwise, crossflow, diffusivity, obstacle, cell_weight):
    adjoint = lax.axis_index("fa").astype(jnp.int32)
    _, inputs, rows, cols = init_fields.shape
    field = tiled(init_fields[0])
    coef_rows = up8(3 * HALO)
    packed_rows = HALO * inputs + coef_rows
    span = rows + 2 * HALO
    half = cols // 2
    vmem = pl.BlockSpec(memory_space=pltpu.VMEM)
    bf16, f32 = jnp.bfloat16, jnp.float32

    packed = jax.ShapeDtypeStruct((packed_rows, cols), bf16)
    up, down = pl.pallas_call(
        functools.partial(pack_kernel, rows, inputs),
        out_shape=(packed, packed),
        in_specs=[vmem] * 5,
        out_specs=(vmem, vmem),
        scratch_shapes=[pltpu.VMEM((coef_rows, cols), f32)],
        name="pack",
    )(field, streamwise, crossflow, diffusivity, obstacle)
    size = lax.axis_size("rows")
    low = lax.ppermute(up, "rows", [(i, i + 1) for i in range(size - 1)])
    high = lax.ppermute(down, "rows", [(i + 1, i) for i in range(size - 1)])

    snaps = jax.ShapeDtypeStruct((NSNAP * inputs, rows * half), bf16)
    grid_rows = pltpu.VMEM((span, cols), f32)
    weights = pltpu.VMEM((cols // LANES * span, LANES), f32)
    final, kept, sent = pl.pallas_call(
        functools.partial(march_kernel, rows, inputs),
        out_shape=(jax.ShapeDtypeStruct(field.shape, f32), snaps, snaps),
        in_specs=[pl.BlockSpec(memory_space=pltpu.SMEM)] + [vmem] * 8,
        out_specs=(vmem,) * 3,
        scratch_shapes=[
            *[pltpu.VMEM((span * inputs, cols), f32)] * 2,
            pltpu.VMEM((coef_rows, cols), f32),
            *[grid_rows] * 3,
            *[weights] * 5,
            pltpu.VMEM((cols // LANES * rows, LANES), f32),
        ],
        name="march",
    )(adjoint[None], field, streamwise, crossflow, diffusivity, obstacle, cell_weight, low, high)

    other = lax.ppermute(sent, "fa", [(0, 1), (1, 0)])
    product = lax.dot_general(kept, other, (((1,), (1,)), ((), ())), preferred_element_type=f32)
    total = jnp.where(adjoint == 1, product, product.T)
    total = total + lax.ppermute(total, "fa", [(0, 1), (1, 0)])
    if size & (size - 1) == 0:
        stride = 1
        while stride < size:
            total = total + lax.ppermute(total, "rows", [(i, i ^ stride) for i in range(size)])
            stride *= 2
    else:
        total = lax.psum(total, "rows")
    hankel = total * (1.0 / math.sqrt(rows * size * cols))
    return (untiled(final, init_fields.shape[1:])[None], hankel)


def solution(mesh):
    placed = (
        P("fa", "ens", "rows", None),
        P("rows", None),
        P("rows", None),
        P("rows", None),
        P("rows", None),
        P("rows", None),
    )
    return jax.shard_map(
        local,
        mesh=mesh,
        in_specs=placed,
        out_specs=(P("fa", "ens", "rows", None), P("ens", None)),
        check_vma=False,
    )
```

```python
import functools
import math

import jax
import jax.numpy as jnp
from jax import lax
from jax.experimental import pallas as pl
from jax.experimental.pallas import tpu as pltpu
from jax.sharding import PartitionSpec as P

NSNAP = 4
STRIDE = 3
HALO = NSNAP * STRIDE
LANES = 128
SUB = 8
PAIR = 2 * LANES
F32 = jnp.float32
BF16 = jnp.bfloat16


def up8(count):
    return -(-count // SUB) * SUB


def lanes_of(tile):
    return slice(tile * LANES, (tile + 1) * LANES)


def tiled(array):
    inputs, rows, cols = array.shape
    split = array.reshape(inputs, rows // SUB, SUB, cols // LANES, LANES)
    return split.transpose(0, 1, 3, 2, 4).reshape(-1, LANES)


def untiled(array, shape):
    inputs, rows, cols = shape
    split = array.reshape(inputs, rows // SUB, cols // LANES, SUB, LANES)
    return split.transpose(0, 1, 3, 2, 4).reshape(shape)


def tile_of(rows, cols, row, tile, inputs):
    start = (row // SUB * (cols // LANES) + tile) * SUB + row % SUB
    return pl.ds(start, inputs, stride=rows * cols // LANES)


def sorting_matrix(back=False):
    source = lax.broadcasted_iota(jnp.int32, (PAIR, PAIR), 1 if back else 0)
    target = lax.broadcasted_iota(jnp.int32, (PAIR, PAIR), 0 if back else 1)
    wanted = jnp.where(target < LANES, 2 * target, 2 * (target - LANES) + 1)
    return jnp.where(source == wanted, 1.0, 0.0).astype(BF16)


def moved(part, matrix):
    return jnp.dot(part, matrix, preferred_element_type=F32)


def moved_whole(values, matrix):
    top = values.astype(BF16)
    rest = values - top.astype(F32)
    middle = rest.astype(BF16)
    bottom = (rest - middle.astype(F32)).astype(BF16)
    return (moved(top, matrix) + moved(middle, matrix)) + moved(bottom, matrix)


def eastern(tiles, tile, lane, count):
    if tile % 2 == 0:
        return tiles[tile + 1]
    after = tiles[(tile + 1) % count]
    return pltpu.roll(jnp.where(lane == 0, after, tiles[tile - 1]), LANES - 1, 1)


def western(tiles, tile, lane, count):
    if tile % 2 == 1:
        return tiles[tile - 1]
    before = tiles[(tile - 1) % count]
    return pltpu.roll(jnp.where(lane == LANES - 1, before, tiles[tile + 1]), 1, 1)


def weights_of(along, across, signed, is_adjoint):
    lane = lax.broadcasted_iota(jnp.int32, along[0].shape, 1)
    count = len(along)
    east, west, north, south, centre = [], [], [], [], []
    for tile in range(count):
        opened = jnp.where(signed[tile] < 0, 0.0, 1.0)
        spread = jnp.abs(signed[tile])
        half_x, half_y = along[tile] * 0.5, across[tile] * 0.5
        east.append(opened * (spread - half_x))
        west.append(opened * (spread + half_x))
        low, high = opened * (spread - half_y), opened * (spread + half_y)
        north.append(jnp.where(is_adjoint, high, low))
        south.append(jnp.where(is_adjoint, low, high))
        centre.append(opened * (1.0 - 4.0 * spread))
    east_w = [jnp.where(is_adjoint, eastern(west, t, lane, count), east[t]) for t in range(count)]
    west_w = [jnp.where(is_adjoint, western(east, t, lane, count), west[t]) for t in range(count)]
    east_w[-1] = jnp.where(lane == LANES - 1, 0.0, east_w[-1])
    west_w[0] = jnp.where(lane == 0, 0.0, west_w[0])
    return east_w, west_w, north, south, centre


def pack_kernel(rows, inputs, field, along, across, viscous, solid, up, down, coefs):
    cols = along.shape[1]
    signed = jnp.where(solid[...] != 0, -viscous[...], viscous[...])
    for out, first in ((up, rows - HALO), (down, 0)):
        for step in range(HALO):
            for tile in range(cols // LANES):
                part = field[tile_of(rows, cols, first + step, tile, inputs), :]
                out[step * inputs : (step + 1) * inputs, lanes_of(tile)] = part.astype(out.dtype)
        coefs[0:HALO, :] = along[first : first + HALO, :]
        coefs[HALO : 2 * HALO, :] = across[first : first + HALO, :]
        coefs[2 * HALO : 3 * HALO, :] = signed[first : first + HALO]
        out[HALO * inputs :, :] = coefs[...].astype(out.dtype)


def prepare_kernel(
    rows, inputs, adjoint_ref, field, along, across, viscous, solid, area, own, weights, scale, lined
):
    is_adjoint = adjoint_ref[0] == 1
    cols = along.shape[1]
    matrix = sorting_matrix()
    for row in range(rows):
        for tile in range(cols // LANES):
            lined[row * inputs : (row + 1) * inputs, lanes_of(tile)] = field[
                tile_of(rows, cols, row, tile, inputs), :
            ]
    signed = jnp.where(solid[...] != 0, -viscous[...], viscous[...])
    factor = jnp.where(is_adjoint, area[...], 1.0)
    sorted_coefs = [[], [], []]
    for pair in range(cols // PAIR):
        at = slice(pair * PAIR, (pair + 1) * PAIR)
        own[:, at] = moved_whole(lined[:, at], matrix)
        for kept, values in zip(sorted_coefs, (along[:, at], across[:, at], signed[:, at])):
            values = moved_whole(values, matrix)
            kept += [values[:, :LANES], values[:, LANES:]]
        values = moved_whole(factor[:, at], matrix)
        for side in range(2):
            tile = 2 * pair + side
            scale[tile * rows : (tile + 1) * rows, :] = values[:, lanes_of(side)]
    for index, tiles in enumerate(weights_of(*sorted_coefs, is_adjoint)):
        for tile, values in enumerate(tiles):
            weights[index, tile * rows : (tile + 1) * rows, :] = values


def march_kernel(
    rows, inputs, adjoint_ref, own, own_weights, scale, low, high,
    final, kept, sent,
    state_a, state_b, coefs, east_w, west_w, north_w, south_w, centre_w,
):
    adjoint = adjoint_ref[0]
    is_adjoint = adjoint == 1
    cols = own.shape[1]
    half = cols // 2
    span = rows + 2 * HALO
    wide = span + 2 * SUB
    tiles = cols // LANES
    matrix = sorting_matrix()
    all_weights = (east_w, west_w, north_w, south_w, centre_w)

    for source, first in ((low, 0), (high, HALO + rows)):
        sorted_coefs = [[], [], []]
        for pair in range(cols // PAIR):
            at = slice(pair * PAIR, (pair + 1) * PAIR)
            values = moved(source[:, at], matrix)
            state_a[(1 + first) * inputs : (1 + first + HALO) * inputs, at] = values[: HALO * inputs]
            coefs[:, at] = values[HALO * inputs :]
            for index, taken in enumerate(sorted_coefs):
                part = coefs[index * HALO : (index + 1) * HALO, at]
                taken += [part[:, :LANES], part[:, LANES:]]
        for ref, values in zip(all_weights, weights_of(*sorted_coefs, is_adjoint)):
            for tile in range(tiles):
                start = tile * wide + SUB + first
                ref[start : start + HALO, :] = values[tile]
    state_a[(1 + HALO) * inputs : (1 + HALO + rows) * inputs, :] = own[...]
    for index, ref in enumerate(all_weights):
        for tile in range(tiles):
            start = tile * wide + SUB + HALO
            ref[start : start + rows, :] = own_weights[index, tile * rows : (tile + 1) * rows, :]

    states = (state_a, state_b)
    lane = lax.broadcasted_iota(jnp.int32, (inputs, LANES), 1)
    for step in range(1, HALO + 1):
        src, dst = states[(step - 1) % 2], states[step % 2]
        count = span - 2 * step
        group = min((8, 7, 9, 10, 6, 11), key=lambda size: -(-count // size) * size)
        trips = -(-count // group)
        first_row = step - (trips * group - count) // 2

        def advance(index, carry, src=src, dst=dst, first_row=first_row, group=group):
            row0 = first_row + index * group

            def at_row(row):
                return pl.ds(pl.multiple_of((1 + row) * inputs, inputs), inputs)

            def weight(ref, row, tile):
                return ref[pl.ds(tile * wide + SUB + row, inputs, stride=0), :]

            lines = [{} for _ in range(group + 2)]
            for pair in range(tiles // 2):
                for n, line in enumerate(lines):
                    for tile in (2 * pair - 1, 2 * pair, 2 * pair + 1, 2 * pair + 2):
                        tile %= tiles
                        if tile not in line and (tile // 2 == pair or 0 < n <= group):
                            line[tile] = src[at_row(row0 + n - 1), lanes_of(tile)]
                for n in range(group):
                    row = row0 + n
                    here = lines[n + 1]
                    for tile in (2 * pair, 2 * pair + 1):
                        total = weight(centre_w, row, tile) * here[tile]
                        total += weight(north_w, row + adjoint, tile) * lines[n + 2][tile]
                        total += weight(south_w, row - adjoint, tile) * lines[n][tile]
                        total += weight(east_w, row, tile) * eastern(here, tile, lane, tiles)
                        total += weight(west_w, row, tile) * western(here, tile, lane, tiles)
                        dst[at_row(row), lanes_of(tile)] = total
            return carry

        lax.fori_loop(0, trips, advance, 0)
        if step % STRIDE == 0:
            snap = slice((step // STRIDE - 1) * inputs, (step // STRIDE) * inputs)

            def record(first, second, scaled, dst=dst, snap=snap):
                for row in range(rows):
                    at = slice((1 + HALO + row) * inputs, (2 + HALO + row) * inputs)
                    for tile in range(tiles):
                        value = dst[at, lanes_of(tile)]
                        if scaled:
                            value = value * scale[pl.ds(tile * rows + row, inputs, stride=0), :]
                        out = first if tile < tiles // 2 else second
                        start = row * half + tile % (tiles // 2) * LANES
                        out[snap, start : start + LANES] = value.astype(out.dtype)

            @pl.when(is_adjoint)
            def _():
                record(sent, kept, True)

            @pl.when(jnp.logical_not(is_adjoint))
            def _():
                record(kept, sent, False)

    final[...] = states[HALO % 2][(1 + HALO) * inputs : (1 + HALO + rows) * inputs, :]


def finish_kernel(rows, inputs, last, final):
    cols = last.shape[1]
    matrix = sorting_matrix(back=True)
    for pair in range(cols // PAIR):
        values = moved_whole(last[:, pair * PAIR : (pair + 1) * PAIR], matrix)
        for row in range(rows):
            for side in range(2):
                final[tile_of(rows, cols, row, 2 * pair + side, inputs), :] = values[
                    row * inputs : (row + 1) * inputs, lanes_of(side)
                ]


def local(init_fields, streamwise, crossflow, diffusivity, obstacle, cell_weight):
    adjoint = lax.axis_index("fa").astype(jnp.int32)
    flag = adjoint[None]
    _, inputs, rows, cols = init_fields.shape
    field = tiled(init_fields[0])
    coef_rows = up8(3 * HALO)
    packed_rows = HALO * inputs + coef_rows
    span = rows + 2 * HALO
    half = cols // 2
    tiles = cols // LANES
    vmem = pl.BlockSpec(memory_space=pltpu.VMEM)
    smem = pl.BlockSpec(memory_space=pltpu.SMEM)

    def shape(*dims, dtype=F32):
        return jax.ShapeDtypeStruct(dims, dtype)

    def cost(amount):
        return pl.CostEstimate(flops=amount, bytes_accessed=4 * field.size * 4, transcendentals=0)

    params = pltpu.CompilerParams(vmem_limit_bytes=24 << 20)
    packed = shape(packed_rows, cols, dtype=BF16)
    up, down = pl.pallas_call(
        functools.partial(pack_kernel, rows, inputs),
        out_shape=(packed, packed),
        in_specs=[vmem] * 5,
        out_specs=(vmem, vmem),
        scratch_shapes=[pltpu.VMEM((coef_rows, cols), F32)],
        compiler_params=params,
        name="pack",
    )(field, streamwise, crossflow, diffusivity, obstacle)
    size = lax.axis_size("rows")
    low = lax.ppermute(up, "rows", [(i, i + 1) for i in range(size - 1)])
    high = lax.ppermute(down, "rows", [(i + 1, i) for i in range(size - 1)])

    own, own_weights, scale = pl.pallas_call(
        functools.partial(prepare_kernel, rows, inputs),
        out_shape=(
            shape(rows * inputs, cols),
            shape(5, tiles * rows, LANES),
            shape(tiles * rows, LANES),
        ),
        in_specs=[smem] + [vmem] * 6,
        out_specs=(vmem,) * 3,
        scratch_shapes=[pltpu.VMEM((rows * inputs, cols), F32)],
        compiler_params=params,
        cost_estimate=cost(10**9),
        name="prepare",
    )(flag, field, streamwise, crossflow, diffusivity, obstacle, cell_weight)

    snaps = shape(NSNAP * inputs, rows * half, dtype=BF16)
    last, kept, sent = pl.pallas_call(
        functools.partial(march_kernel, rows, inputs),
        out_shape=(shape(rows * inputs, cols), snaps, snaps),
        in_specs=[smem] + [vmem] * 5,
        out_specs=(vmem,) * 3,
        scratch_shapes=[
            *[pltpu.VMEM(((span + 2) * inputs, cols), F32)] * 2,
            pltpu.VMEM((coef_rows, cols), F32),
            *[pltpu.VMEM((tiles * (span + 2 * SUB), LANES), F32)] * 5,
        ],
        compiler_params=params,
        name="march",
    )(flag, own, own_weights, scale, low, high)

    other = lax.ppermute(sent, "fa", [(0, 1), (1, 0)])
    product = lax.dot_general(kept, other, (((1,), (1,)), ((), ())), preferred_element_type=F32)
    total = jnp.where(adjoint == 1, product, product.T)
    total = total + lax.ppermute(total, "fa", [(0, 1), (1, 0)])
    if size & (size - 1) == 0:
        stride = 1
        while stride < size:
            total = total + lax.ppermute(total, "rows", [(i, i ^ stride) for i in range(size)])
            stride *= 2
    else:
        total = lax.psum(total, "rows")
    hankel = total * (1.0 / math.sqrt(rows * size * cols))
    final = pl.pallas_call(
        functools.partial(finish_kernel, rows, inputs),
        out_shape=shape(*field.shape),
        in_specs=[vmem],
        out_specs=vmem,
        compiler_params=params,
        cost_estimate=cost(10**7),
        name="finish",
    )(last)
    return (untiled(final, init_fields.shape[1:])[None], hankel)


def solution(mesh):
    placed = (
        P("fa", "ens", "rows", None),
        P("rows", None),
        P("rows", None),
        P("rows", None),
        P("rows", None),
        P("rows", None),
    )
    return jax.shard_map(
        local,
        mesh=mesh,
        in_specs=placed,
        out_specs=(P("fa", "ens", "rows", None), P("ens", None)),
        check_vma=False,
    )
```

```python
import functools
import math

import jax
import jax.numpy as jnp
from jax import lax
from jax.experimental import pallas as pl
from jax.experimental.pallas import tpu as pltpu
from jax.sharding import PartitionSpec as P


NSNAP = 4
STRIDE = 3
HALO = NSNAP * STRIDE
LANES = 128
SUB = 8
PAIR = 2 * LANES
F32 = jnp.float32
BF16 = jnp.bfloat16


def up8(count):
    return -(-count // SUB) * SUB


def lanes_of(tile):
    return slice(tile * LANES, (tile + 1) * LANES)


def tiled(array):
    inputs, rows, cols = array.shape
    split = array.reshape(inputs, rows // SUB, SUB, cols // LANES, LANES)
    return split.transpose(0, 1, 3, 2, 4).reshape(-1, LANES)


def untiled(array, shape):
    inputs, rows, cols = shape
    split = array.reshape(inputs, rows // SUB, cols // LANES, SUB, LANES)
    return split.transpose(0, 1, 3, 2, 4).reshape(shape)


def tile_of(rows, cols, row, tile, inputs):
    start = (row // SUB * (cols // LANES) + tile) * SUB + row % SUB
    return pl.ds(start, inputs, stride=rows * cols // LANES)


def sorting_matrix(back=False):
    source = lax.broadcasted_iota(jnp.int32, (PAIR, PAIR), 1 if back else 0)
    target = lax.broadcasted_iota(jnp.int32, (PAIR, PAIR), 0 if back else 1)
    wanted = jnp.where(target < LANES, 2 * target, 2 * (target - LANES) + 1)
    return jnp.where(source == wanted, 1.0, 0.0).astype(BF16)


def moved(part, matrix):
    return jnp.dot(part, matrix, preferred_element_type=F32)


def moved_whole(values, matrix):
    top = values.astype(BF16)
    rest = values - top.astype(F32)
    middle = rest.astype(BF16)
    bottom = (rest - middle.astype(F32)).astype(BF16)
    return (moved(top, matrix) + moved(middle, matrix)) + moved(bottom, matrix)


def eastern(tiles, tile, lane, count):
    if tile % 2 == 0:
        return tiles[tile + 1]
    after = tiles[(tile + 1) % count]
    return pltpu.roll(jnp.where(lane == 0, after, tiles[tile - 1]), LANES - 1, 1)


def western(tiles, tile, lane, count):
    if tile % 2 == 1:
        return tiles[tile - 1]
    before = tiles[(tile - 1) % count]
    return pltpu.roll(jnp.where(lane == LANES - 1, before, tiles[tile + 1]), 1, 1)


def weights_of(along, across, signed, is_adjoint, first_col=True, last_col=True):
    lane = lax.broadcasted_iota(jnp.int32, along[0].shape, 1)
    count = len(along)
    east, west, north, south, centre = [], [], [], [], []
    for tile in range(count):
        opened = jnp.where(signed[tile] < 0, 0.0, 1.0)
        spread = jnp.abs(signed[tile])
        half_x, half_y = along[tile] * 0.5, across[tile] * 0.5
        east.append(opened * (spread - half_x))
        west.append(opened * (spread + half_x))
        low, high = opened * (spread - half_y), opened * (spread + half_y)
        north.append(jnp.where(is_adjoint, high, low))
        south.append(jnp.where(is_adjoint, low, high))
        centre.append(opened * (1.0 - 4.0 * spread))
    east_w = [jnp.where(is_adjoint, eastern(west, t, lane, count), east[t]) for t in range(count)]
    west_w = [jnp.where(is_adjoint, western(east, t, lane, count), west[t]) for t in range(count)]
    if last_col:
        east_w[-1] = jnp.where(lane == LANES - 1, 0.0, east_w[-1])
    if first_col:
        west_w[0] = jnp.where(lane == 0, 0.0, west_w[0])
    return east_w, west_w, north, south, centre


def pack_kernel(
    rows, inputs, cuts, field_in, along_in, across_in, viscous_in, solid_in, *refs
):
    outs, (coefs, field, along, across, viscous, solid, sems) = refs[:-7], refs[-7:]
    cols = along.shape[1]
    copies = [
        pltpu.make_async_copy(source, target, sems.at[index])
        for index, (source, target) in enumerate(
            (
                (field_in, field),
                (along_in, along),
                (across_in, across),
                (viscous_in, viscous),
                (solid_in, solid),
            )
        )
    ]
    for copy in copies:
        copy.start()
    for copy in copies:
        copy.wait()
    signed = jnp.where(solid[...] != 0, -viscous[...], viscous[...])
    for side, first in enumerate((rows - HALO, 0)):
        coefs[0:HALO, :] = along[first : first + HALO, :]
        coefs[HALO : 2 * HALO, :] = across[first : first + HALO, :]
        coefs[2 * HALO : 3 * HALO, :] = signed[first : first + HALO]
        for chunk, (left, right) in enumerate(cuts):
            out = outs[2 * chunk + side]
            for step in range(HALO):
                for tile in range(left // LANES, right // LANES):
                    part = field[tile_of(rows, cols, first + step, tile, inputs), :]
                    to = lanes_of(tile - left // LANES)
                    out[step * inputs : (step + 1) * inputs, to] = part.astype(out.dtype)
            out[HALO * inputs :, :] = coefs[:, left:right].astype(out.dtype)


def prepare_kernel(
    rows, inputs, adjoint_ref, field, along, across, viscous, solid, area, own, weights, scale, lined
):
    is_adjoint = adjoint_ref[0] == 1
    cols = along.shape[1]
    matrix = sorting_matrix()
    for row in range(rows):
        for tile in range(cols // LANES):
            lined[row * inputs : (row + 1) * inputs, lanes_of(tile)] = field[
                tile_of(rows, cols, row, tile, inputs), :
            ]
    signed = jnp.where(solid[...] != 0, -viscous[...], viscous[...])
    factor = jnp.where(is_adjoint, area[...], 1.0)
    sorted_coefs = [[], [], []]
    for pair in range(cols // PAIR):
        at = slice(pair * PAIR, (pair + 1) * PAIR)
        own[:, at] = moved_whole(lined[:, at], matrix)
        for kept, values in zip(sorted_coefs, (along[:, at], across[:, at], signed[:, at])):
            values = moved_whole(values, matrix)
            kept += [values[:, :LANES], values[:, LANES:]]
        values = moved_whole(factor[:, at], matrix)
        for side in range(2):
            tile = 2 * pair + side
            scale[tile * rows : (tile + 1) * rows, :] = values[:, lanes_of(side)]
    for index, tiles in enumerate(weights_of(*sorted_coefs, is_adjoint)):
        for tile, values in enumerate(tiles):
            weights[index, tile * rows : (tile + 1) * rows, :] = values


def march_kernel(rows, inputs, first_pair, last_pair, sources, owned, all_pairs, adjoint_ref, own, own_weights, scale, *refs):
    count = 2 * (1 + max(operand for operand, _ in sources))
    halos, refs = refs[:count], refs[count:]
    if last_pair < all_pairs:
        for side in range(2):
            refs[3][side] = halos[side][:, (last_pair - 1 - first_pair) * PAIR :]
        refs = (*refs[:3], *refs[4:])
    last, kept, sent, state_a, state_b, coefs, east_w, west_w, north_w, south_w, centre_w = refs
    adjoint = adjoint_ref[0]
    is_adjoint = adjoint == 1
    tiles = 2 * (last_pair - first_pair)
    tile0 = 2 * first_pair
    span = rows + 2 * HALO
    wide = span + 2 * SUB
    matrix = sorting_matrix()
    all_weights = (east_w, west_w, north_w, south_w, centre_w)
    edges = (first_pair == 0, last_pair == all_pairs)

    for side, first in ((0, 0), (1, HALO + rows)):
        sorted_coefs = [[], [], []]
        for pair, (operand, place) in enumerate(sources):
            at = slice(pair * PAIR, (pair + 1) * PAIR)
            source = halos[2 * operand + side]
            values = moved(source[:, place * PAIR : (place + 1) * PAIR], matrix)
            state_a[(1 + first) * inputs : (1 + first + HALO) * inputs, at] = values[: HALO * inputs]
            coefs[:, at] = values[HALO * inputs :]
            for index, taken in enumerate(sorted_coefs):
                part = coefs[index * HALO : (index + 1) * HALO, at]
                taken += [part[:, :LANES], part[:, LANES:]]
        for ref, values in zip(all_weights, weights_of(*sorted_coefs, is_adjoint, *edges)):
            for tile in range(tiles):
                start = tile * wide + SUB + first
                ref[start : start + HALO, :] = values[tile]
    state_a[(1 + HALO) * inputs : (1 + HALO + rows) * inputs, :] = own[
        :, tile0 * LANES : (tile0 + tiles) * LANES
    ]
    for index, ref in enumerate(all_weights):
        for tile in range(tiles):
            start = tile * wide + SUB + HALO
            at = slice((tile0 + tile) * rows, (tile0 + tile + 1) * rows)
            ref[start : start + rows, :] = own_weights[index, at, :]

    states = (state_a, state_b)
    lane = lax.broadcasted_iota(jnp.int32, (inputs, LANES), 1)
    for step in range(1, HALO + 1):
        src, dst = states[(step - 1) % 2], states[step % 2]
        count = span - 2 * step
        group = min((8, 7, 9, 10, 6, 11), key=lambda size: -(-count // size) * size)
        trips = -(-count // group)
        first_row = step - (trips * group - count) // 2

        def advance(index, carry, src=src, dst=dst, first_row=first_row, group=group):
            row0 = first_row + index * group

            def at_row(row):
                return pl.ds(pl.multiple_of((1 + row) * inputs, inputs), inputs)

            def weight(ref, row, tile):
                return ref[pl.ds(tile * wide + SUB + row, inputs, stride=0), :]

            lines = [{} for _ in range(group + 2)]
            for pair in range(tiles // 2):
                for n, line in enumerate(lines):
                    for tile in (2 * pair - 1, 2 * pair, 2 * pair + 1, 2 * pair + 2):
                        tile %= tiles
                        if tile not in line and (tile // 2 == pair or 0 < n <= group):
                            line[tile] = src[at_row(row0 + n - 1), lanes_of(tile)]
                for n in range(group):
                    row = row0 + n
                    here = lines[n + 1]
                    for tile in (2 * pair, 2 * pair + 1):
                        total = weight(centre_w, row, tile) * here[tile]
                        total += weight(north_w, row + adjoint, tile) * lines[n + 2][tile]
                        total += weight(south_w, row - adjoint, tile) * lines[n][tile]
                        total += weight(east_w, row, tile) * eastern(here, tile, lane, tiles)
                        total += weight(west_w, row, tile) * western(here, tile, lane, tiles)
                        dst[at_row(row), lanes_of(tile)] = total
            return carry

        lax.fori_loop(0, trips, advance, 0)
        if step % STRIDE == 0:
            snap = slice((step // STRIDE - 1) * inputs, (step // STRIDE) * inputs)

            def record(first, second, scaled, dst=dst, snap=snap):
                for row in range(rows):
                    at = slice((1 + HALO + row) * inputs, (2 + HALO + row) * inputs)
                    for tile in range(tiles):
                        value = dst[at, lanes_of(tile)]
                        if scaled:
                            factor = pl.ds((tile0 + tile) * rows + row, inputs, stride=0)
                            value = value * scale[factor, :]
                        low_lane, high_lane = 0, LANES
                        if tile < 2:
                            low_lane = owned[0]
                        if tile >= tiles - 2:
                            high_lane = owned[1]
                        if low_lane > 0:
                            value = jnp.where(lane >= low_lane, value, 0.0)
                        if high_lane < LANES:
                            value = jnp.where(lane < high_lane, value, 0.0)
                        out = first if tile < tiles // 2 else second
                        start = (row * (tiles // 2) + tile % (tiles // 2)) * LANES
                        out[snap, start : start + LANES] = value.astype(out.dtype)

            @pl.when(is_adjoint)
            def _():
                record(sent, kept, True)

            @pl.when(jnp.logical_not(is_adjoint))
            def _():
                record(kept, sent, False)

    last[...] = states[HALO % 2][(1 + HALO) * inputs : (1 + HALO + rows) * inputs, :]


def meet_kernel(adjoint_ref, mine_a, other_a, mine_b, other_b, product):
    def met(rows, columns):
        return lax.dot_general(
            rows[...], columns[...], (((1,), (1,)), ((), ())), preferred_element_type=F32
        )

    @pl.when(adjoint_ref[0] == 0)
    def _():
        product[...] = met(other_a, mine_a) + met(other_b, mine_b)

    @pl.when(adjoint_ref[0] != 0)
    def _():
        product[...] = met(mine_a, other_a) + met(mine_b, other_b)


def finish_kernel(rows, inputs, shared, left, right, final):
    matrix = sorting_matrix(back=True)
    lane = lax.broadcasted_iota(jnp.int32, (rows * inputs, PAIR), 1)
    pairs = shared + right.shape[1] // PAIR
    for pair in range(pairs):
        if pair <= shared:
            values = left[:, pair * PAIR : (pair + 1) * PAIR]
        if pair >= shared:
            others = right[:, (pair - shared) * PAIR : (pair - shared + 1) * PAIR]
            values = jnp.where(lane % LANES < LANES // 2, values, others) if pair == shared else others
        values = moved_whole(values, matrix)
        for row in range(rows):
            for side in range(2):
                final[tile_of(rows, pairs * PAIR, row, 2 * pair + side, inputs), :] = values[
                    row * inputs : (row + 1) * inputs, lanes_of(side)
                ]


def local(init_fields, streamwise, crossflow, diffusivity, obstacle, cell_weight):
    adjoint = lax.axis_index("fa").astype(jnp.int32)
    flag = adjoint[None]
    _, inputs, rows, cols = init_fields.shape
    field = tiled(init_fields[0])
    coef_rows = up8(3 * HALO)
    packed_rows = HALO * inputs + coef_rows
    span = rows + 2 * HALO
    tiles = cols // LANES
    vmem = pl.BlockSpec(memory_space=pltpu.VMEM)
    smem = pl.BlockSpec(memory_space=pltpu.SMEM)

    def shape(*dims, dtype=F32):
        return jax.ShapeDtypeStruct(dims, dtype)

    def cost(amount):
        return pl.CostEstimate(flops=amount, bytes_accessed=4 * field.size * 4, transcendentals=0)

    params = pltpu.CompilerParams(vmem_limit_bytes=14 << 20)
    hbm = pl.BlockSpec(memory_space=pltpu.HBM)
    pairs = cols // PAIR
    shared = pairs // 2
    cut = (shared + 1) * PAIR
    cuts = ((0, cut), (cut, cols))
    packed = [
        shape(packed_rows, right - left, dtype=BF16) for left, right in cuts for _ in range(2)
    ]
    plane = pltpu.VMEM((rows, cols), F32)
    up_a, down_a, up_b, down_b = pl.pallas_call(
        functools.partial(pack_kernel, rows, inputs, cuts),
        out_shape=packed,
        in_specs=[hbm] * 5,
        out_specs=[vmem] * 4,
        scratch_shapes=[
            pltpu.VMEM((coef_rows, cols), F32),
            pltpu.VMEM(field.shape, F32),
            plane,
            plane,
            plane,
            pltpu.VMEM((rows, cols), jnp.int32),
            pltpu.SemaphoreType.DMA((5,)),
        ],
        compiler_params=params,
        name="pack",
    )(*[pltpu.with_memory_space_constraint(x, pltpu.HBM) for x in (field, streamwise, crossflow, diffusivity, obstacle)])
    size = lax.axis_size("rows")
    rise = [(i, i + 1) for i in range(size - 1)]
    fall = [(j, i) for i, j in rise]
    low_a, high_a = lax.ppermute(up_a, "rows", rise), lax.ppermute(down_a, "rows", fall)
    low_b, high_b = lax.ppermute(up_b, "rows", rise), lax.ppermute(down_b, "rows", fall)

    prepare = pl.pallas_call(
        functools.partial(prepare_kernel, rows, inputs),
        out_shape=(
            shape(rows * inputs, cols),
            shape(5, tiles * rows, LANES),
            shape(tiles * rows, LANES),
        ),
        in_specs=[smem] + [vmem] * 6,
        out_specs=(vmem,) * 3,
        scratch_shapes=[pltpu.VMEM((rows * inputs, cols), F32)],
        compiler_params=params,
        cost_estimate=cost(10**9),
        name="prepare",
    )
    own, own_weights, scale = prepare(
        flag, field, streamwise, crossflow, diffusivity, obstacle, cell_weight
    )

    def march(first_pair, last_pair, sources, owned, halos):
        more = [shape(2, packed_rows, PAIR, dtype=BF16)] * (last_pair < pairs)
        chunk = (last_pair - first_pair) * PAIR
        return pl.pallas_call(
            functools.partial(
                march_kernel, rows, inputs, first_pair, last_pair, sources, owned, pairs
            ),
            out_shape=(
                shape(rows * inputs, chunk),
                *[shape(NSNAP * inputs, rows * chunk // 2, dtype=BF16)] * 2,
                *more,
            ),
            in_specs=[smem] + [vmem] * (3 + len(halos)),
            out_specs=(vmem,) * (3 + len(more)),
            scratch_shapes=[
                *[pltpu.VMEM(((span + 2) * inputs, chunk), F32)] * 2,
                pltpu.VMEM((coef_rows, chunk), F32),
                *[pltpu.VMEM((chunk // LANES * (span + 2 * SUB), LANES), F32)] * 5,
            ],
            compiler_params=params,
            cost_estimate=cost(10**9),
        )(flag, own, own_weights, scale, *halos)

    middle = LANES // 2
    last_a, kept_a, sent_a, both = march(
        0, shared + 1, [(0, p) for p in range(shared + 1)], (0, middle), (low_a, high_a)
    )
    last_b, kept_b, sent_b = march(
        shared,
        pairs,
        [(0, 0)] + [(1, p) for p in range(pairs - shared - 1)],
        (middle, LANES),
        (both[0], both[1], low_b, high_b),
    )
    swap = [(0, 1), (1, 0)]
    other_a = lax.ppermute(sent_a, "fa", swap)
    other_b = lax.ppermute(sent_b, "fa", swap)
    total = pl.pallas_call(
        meet_kernel,
        out_shape=shape(NSNAP * inputs, NSNAP * inputs),
        in_specs=[smem] + [vmem] * 4,
        out_specs=vmem,
        compiler_params=params,
        name="meet",
    )(flag, kept_a, other_a, kept_b, other_b)
    total = total + lax.ppermute(total, "fa", swap)
    if size & (size - 1) == 0:
        stride = 1
        while stride < size:
            total = total + lax.ppermute(total, "rows", [(i, i ^ stride) for i in range(size)])
            stride *= 2
    else:
        total = lax.psum(total, "rows")
    hankel = total * (1.0 / math.sqrt(rows * size * cols))
    final = pl.pallas_call(
        functools.partial(finish_kernel, rows, inputs, shared),
        out_shape=shape(*field.shape),
        in_specs=[vmem] * 2,
        out_specs=vmem,
        compiler_params=params,
        cost_estimate=cost(10**7),
        name="finish",
    )(last_a, last_b)
    return (untiled(final, init_fields.shape[1:])[None], hankel)


def solution(mesh):
    placed = (
        P("fa", "ens", "rows", None),
        P("rows", None),
        P("rows", None),
        P("rows", None),
        P("rows", None),
        P("rows", None),
    )

    return jax.shard_map(
        local,
        mesh=mesh,
        in_specs=placed,
        out_specs=(P("fa", "ens", "rows", None), P("ens", None)),
        check_vma=False,
    )
```

```python
import functools
import math

import jax
import jax.numpy as jnp
from jax import lax
from jax.experimental import pallas as pl
from jax.experimental.pallas import tpu as pltpu
from jax.sharding import PartitionSpec as P


NSNAP = 4
STRIDE = 3
HALO = NSNAP * STRIDE
LANES = 128
SUB = 8
PAIR = 2 * LANES
F32 = jnp.float32
BF16 = jnp.bfloat16


def up8(count):
    return -(-count // SUB) * SUB


def lanes_of(tile):
    return slice(tile * LANES, (tile + 1) * LANES)


def tiled(array):
    inputs, rows, cols = array.shape
    split = array.reshape(inputs, rows // SUB, SUB, cols // LANES, LANES)
    return split.transpose(0, 1, 3, 2, 4).reshape(-1, LANES)


def untiled(array, shape):
    inputs, rows, cols = shape
    split = array.reshape(inputs, rows // SUB, cols // LANES, SUB, LANES)
    return split.transpose(0, 1, 3, 2, 4).reshape(shape)


def tile_of(rows, cols, row, tile, inputs):
    start = (row // SUB * (cols // LANES) + tile) * SUB + row % SUB
    return pl.ds(start, inputs, stride=rows * cols // LANES)


def sorting_matrix(back=False):
    source = lax.broadcasted_iota(jnp.int32, (PAIR, PAIR), 1 if back else 0)
    target = lax.broadcasted_iota(jnp.int32, (PAIR, PAIR), 0 if back else 1)
    wanted = jnp.where(target < LANES, 2 * target, 2 * (target - LANES) + 1)
    return jnp.where(source == wanted, 1.0, 0.0).astype(BF16)


def moved(part, matrix):
    return jnp.dot(part, matrix, preferred_element_type=F32)


def moved_whole(values, matrix):
    top = values.astype(BF16)
    rest = values - top.astype(F32)
    middle = rest.astype(BF16)
    bottom = (rest - middle.astype(F32)).astype(BF16)
    return (moved(top, matrix) + moved(middle, matrix)) + moved(bottom, matrix)


def eastern(tiles, tile, lane, count):
    if tile % 2 == 0:
        return tiles[tile + 1]
    after = tiles[(tile + 1) % count]
    return pltpu.roll(jnp.where(lane == 0, after, tiles[tile - 1]), LANES - 1, 1)


def western(tiles, tile, lane, count):
    if tile % 2 == 1:
        return tiles[tile - 1]
    before = tiles[(tile - 1) % count]
    return pltpu.roll(jnp.where(lane == LANES - 1, before, tiles[tile + 1]), 1, 1)


def weights_of(along, across, signed, is_adjoint, first_col=True, last_col=True):
    lane = lax.broadcasted_iota(jnp.int32, along[0].shape, 1)
    count = len(along)
    east, west, north, south, centre = [], [], [], [], []
    for tile in range(count):
        opened = jnp.where(signed[tile] < 0, 0.0, 1.0)
        spread = jnp.abs(signed[tile])
        half_x, half_y = along[tile] * 0.5, across[tile] * 0.5
        east.append(opened * (spread - half_x))
        west.append(opened * (spread + half_x))
        low, high = opened * (spread - half_y), opened * (spread + half_y)
        north.append(jnp.where(is_adjoint, high, low))
        south.append(jnp.where(is_adjoint, low, high))
        centre.append(opened * (1.0 - 4.0 * spread))
    east_w = [jnp.where(is_adjoint, eastern(west, t, lane, count), east[t]) for t in range(count)]
    west_w = [jnp.where(is_adjoint, western(east, t, lane, count), west[t]) for t in range(count)]
    if last_col:
        east_w[-1] = jnp.where(lane == LANES - 1, 0.0, east_w[-1])
    if first_col:
        west_w[0] = jnp.where(lane == 0, 0.0, west_w[0])
    return east_w, west_w, north, south, centre


def pack_kernel(
    rows, inputs, left, odd_ref, field_in, along_in, across_in, viscous_in, solid_in,
    inner, outer, coefs, field, along, across, viscous, solid, sems,
):
    cols = along.shape[1]
    right = left + inner.shape[1]
    copies = [
        pltpu.make_async_copy(source, target, sems.at[index])
        for index, (source, target) in enumerate(
            (
                (field_in, field),
                (along_in, along),
                (across_in, across),
                (viscous_in, viscous),
                (solid_in, solid),
            )
        )
    ]
    for copy in copies:
        copy.start()
    for copy in copies:
        copy.wait()
    is_odd = odd_ref[0] == 1
    signed = jnp.where(solid[:, left:right] != 0, -viscous[:, left:right], viscous[:, left:right])
    planes = (along[:, left:right], across[:, left:right], signed)

    def fill(out, first):
        for index, plane in enumerate(planes):
            coefs[index * HALO : (index + 1) * HALO, :] = plane[first : first + HALO]
        out[HALO * inputs :, :] = coefs[...].astype(out.dtype)
        for step in range(HALO):
            for tile in range(left // LANES, right // LANES):
                part = field[tile_of(rows, cols, first + step, tile, inputs), :]
                to = lanes_of(tile - left // LANES)
                out[step * inputs : (step + 1) * inputs, to] = part.astype(out.dtype)

    @pl.when(is_odd)
    def _():
        fill(inner, 0)
        fill(outer, rows - HALO)

    @pl.when(jnp.logical_not(is_odd))
    def _():
        fill(inner, rows - HALO)
        fill(outer, 0)


def prepare_kernel(
    rows, inputs, adjoint_ref, field, along, across, viscous, solid, area, own, weights, scale, lined
):
    is_adjoint = adjoint_ref[0] == 1
    cols = along.shape[1]
    matrix = sorting_matrix()
    for row in range(rows):
        for tile in range(cols // LANES):
            lined[row * inputs : (row + 1) * inputs, lanes_of(tile)] = field[
                tile_of(rows, cols, row, tile, inputs), :
            ]
    signed = jnp.where(solid[...] != 0, -viscous[...], viscous[...])
    factor = jnp.where(is_adjoint, area[...], 1.0)
    sorted_coefs = [[], [], []]
    for pair in range(cols // PAIR):
        at = slice(pair * PAIR, (pair + 1) * PAIR)
        own[:, at] = moved_whole(lined[:, at], matrix)
        for kept, values in zip(sorted_coefs, (along[:, at], across[:, at], signed[:, at])):
            values = moved_whole(values, matrix)
            kept += [values[:, :LANES], values[:, LANES:]]
        values = moved_whole(factor[:, at], matrix)
        for side in range(2):
            tile = 2 * pair + side
            scale[tile * rows : (tile + 1) * rows, :] = values[:, lanes_of(side)]
    for index, tiles in enumerate(weights_of(*sorted_coefs, is_adjoint)):
        for tile, values in enumerate(tiles):
            weights[index, tile * rows : (tile + 1) * rows, :] = values


def march_kernel(rows, inputs, first_pair, last_pair, sources, owned, all_pairs, flags, own, own_weights, scale, *refs):
    count = 2 * (1 + max(operand for operand, _ in sources))
    halos, refs = refs[:count], refs[count:]
    both = None
    if last_pair < all_pairs:
        both = refs[3]
        refs = (*refs[:3], *refs[4:])
    last, kept, sent, state_a, state_b, coefs, east_w, west_w, north_w, south_w, centre_w = refs
    adjoint = flags[0]
    is_adjoint = adjoint == 1
    is_odd = flags[1] == 1
    tiles = 2 * (last_pair - first_pair)
    tile0 = 2 * first_pair
    span = rows + 2 * HALO
    wide = span + 2 * SUB
    matrix = sorting_matrix()
    all_weights = (east_w, west_w, north_w, south_w, centre_w)
    edges = (first_pair == 0, last_pair == all_pairs)

    def fill(low_at, high_at):
        for side, first, at_side in ((0, 0, low_at), (1, HALO + rows, high_at)):
            sorted_coefs = [[], [], []]
            for pair, (operand, place) in enumerate(sources):
                at = slice(pair * PAIR, (pair + 1) * PAIR)
                source = halos[2 * operand + at_side[operand]]
                source = source[:, place * PAIR : (place + 1) * PAIR]
                if both is not None and pair == len(sources) - 1:
                    both[side] = source
                values = moved(source, matrix)
                state_a[(1 + first) * inputs : (1 + first + HALO) * inputs, at] = values[
                    : HALO * inputs
                ]
                coefs[:, at] = values[HALO * inputs :]
                for index, taken in enumerate(sorted_coefs):
                    part = coefs[index * HALO : (index + 1) * HALO, at]
                    taken += [part[:, :LANES], part[:, LANES:]]
            for ref, values in zip(all_weights, weights_of(*sorted_coefs, is_adjoint, *edges)):
                for tile in range(tiles):
                    start = tile * wide + SUB + first
                    ref[start : start + HALO, :] = values[tile]

    fixed = (0,) * (len(halos) // 2 - 1), (1,) * (len(halos) // 2 - 1)

    @pl.when(is_odd)
    def _():
        fill((*fixed[0], 0), (*fixed[1], 1))

    @pl.when(jnp.logical_not(is_odd))
    def _():
        fill((*fixed[0], 1), (*fixed[1], 0))

    state_a[(1 + HALO) * inputs : (1 + HALO + rows) * inputs, :] = own[
        :, tile0 * LANES : (tile0 + tiles) * LANES
    ]
    for index, ref in enumerate(all_weights):
        for tile in range(tiles):
            start = tile * wide + SUB + HALO
            at = slice((tile0 + tile) * rows, (tile0 + tile + 1) * rows)
            ref[start : start + rows, :] = own_weights[index, at, :]

    states = (state_a, state_b)
    lane = lax.broadcasted_iota(jnp.int32, (inputs, LANES), 1)
    for step in range(1, HALO + 1):
        src, dst = states[(step - 1) % 2], states[step % 2]

        def line(row, src=src):
            at = slice((1 + row) * inputs, (2 + row) * inputs)
            return [src[at, lanes_of(tile)] for tile in range(tiles)]

        def weight(ref, row, tile):
            return ref[pl.ds(tile * wide + SUB + row, inputs, stride=0), :]

        behind, here = line(step - 1), line(step)
        for row in range(step, span - step):
            ahead = line(row + 1)
            for tile in range(tiles):
                total = weight(centre_w, row, tile) * here[tile]
                total += weight(north_w, row + adjoint, tile) * ahead[tile]
                total += weight(south_w, row - adjoint, tile) * behind[tile]
                total += weight(east_w, row, tile) * eastern(here, tile, lane, tiles)
                total += weight(west_w, row, tile) * western(here, tile, lane, tiles)
                dst[(1 + row) * inputs : (2 + row) * inputs, lanes_of(tile)] = total
            behind, here = here, ahead
        if step % STRIDE == 0:
            snap = slice((step // STRIDE - 1) * inputs, (step // STRIDE) * inputs)

            def record(first, second, scaled, dst=dst, snap=snap):
                for row in range(rows):
                    at = slice((1 + HALO + row) * inputs, (2 + HALO + row) * inputs)
                    for tile in range(tiles):
                        value = dst[at, lanes_of(tile)]
                        if scaled:
                            factor = pl.ds((tile0 + tile) * rows + row, inputs, stride=0)
                            value = value * scale[factor, :]
                        low_lane, high_lane = 0, LANES
                        if tile < 2:
                            low_lane = owned[0]
                        if tile >= tiles - 2:
                            high_lane = owned[1]
                        if low_lane > 0:
                            value = jnp.where(lane >= low_lane, value, 0.0)
                        if high_lane < LANES:
                            value = jnp.where(lane < high_lane, value, 0.0)
                        out = first if tile < tiles // 2 else second
                        start = (row * (tiles // 2) + tile % (tiles // 2)) * LANES
                        out[snap, start : start + LANES] = value.astype(out.dtype)

            @pl.when(is_adjoint)
            def _():
                record(sent, kept, True)

            @pl.when(jnp.logical_not(is_adjoint))
            def _():
                record(kept, sent, False)

    last[...] = states[HALO % 2][(1 + HALO) * inputs : (1 + HALO + rows) * inputs, :]


def meet_kernel(adjoint_ref, mine_a, other_a, mine_b, other_b, product):
    def met(rows, columns):
        return lax.dot_general(
            rows[...], columns[...], (((1,), (1,)), ((), ())), preferred_element_type=F32
        )

    @pl.when(adjoint_ref[0] == 0)
    def _():
        product[...] = met(other_a, mine_a) + met(other_b, mine_b)

    @pl.when(adjoint_ref[0] != 0)
    def _():
        product[...] = met(mine_a, other_a) + met(mine_b, other_b)


def finish_kernel(rows, inputs, shared, left, right, final):
    matrix = sorting_matrix(back=True)
    lane = lax.broadcasted_iota(jnp.int32, (rows * inputs, PAIR), 1)
    pairs = shared + right.shape[1] // PAIR
    for pair in range(pairs):
        if pair <= shared:
            values = left[:, pair * PAIR : (pair + 1) * PAIR]
        if pair >= shared:
            others = right[:, (pair - shared) * PAIR : (pair - shared + 1) * PAIR]
            values = jnp.where(lane % LANES < LANES // 2, values, others) if pair == shared else others
        values = moved_whole(values, matrix)
        for row in range(rows):
            for side in range(2):
                final[tile_of(rows, pairs * PAIR, row, 2 * pair + side, inputs), :] = values[
                    row * inputs : (row + 1) * inputs, lanes_of(side)
                ]


def local(init_fields, streamwise, crossflow, diffusivity, obstacle, cell_weight):
    adjoint = lax.axis_index("fa").astype(jnp.int32)
    flag = jnp.stack([adjoint, lax.axis_index("rows").astype(jnp.int32) % 2])
    odd = flag[1:]
    _, inputs, rows, cols = init_fields.shape
    field = tiled(init_fields[0])
    coef_rows = up8(3 * HALO)
    packed_rows = HALO * inputs + coef_rows
    span = rows + 2 * HALO
    tiles = cols // LANES
    vmem = pl.BlockSpec(memory_space=pltpu.VMEM)
    smem = pl.BlockSpec(memory_space=pltpu.SMEM)

    def shape(*dims, dtype=F32):
        return jax.ShapeDtypeStruct(dims, dtype)

    def cost(amount):
        return pl.CostEstimate(flops=amount, bytes_accessed=4 * field.size * 4, transcendentals=0)

    params = pltpu.CompilerParams(vmem_limit_bytes=14 << 20)
    hbm = pl.BlockSpec(memory_space=pltpu.HBM)
    pairs = cols // PAIR
    shared = pairs // 2
    cut = (shared + 1) * PAIR
    plane = pltpu.VMEM((rows, cols), F32)
    grids = [
        pltpu.with_memory_space_constraint(x, pltpu.HBM)
        for x in (field, streamwise, crossflow, diffusivity, obstacle)
    ]

    def pack(left, right):
        return pl.pallas_call(
            functools.partial(pack_kernel, rows, inputs, left),
            out_shape=[shape(packed_rows, right - left, dtype=BF16)] * 2,
            in_specs=[smem] + [hbm] * 5,
            out_specs=[vmem] * 2,
            scratch_shapes=[
                pltpu.VMEM((coef_rows, right - left), F32),
                pltpu.VMEM(field.shape, F32),
                plane,
                plane,
                plane,
                pltpu.VMEM((rows, cols), jnp.int32),
                pltpu.SemaphoreType.DMA((5,)),
            ],
            compiler_params=params,
            cost_estimate=cost(10**8),
        )(odd, *grids)

    size = lax.axis_size("rows")
    inner = [(i, i ^ 1) for i in range(size) if i ^ 1 < size]
    outer = [(i, (i - 1 ^ 1) + 1) for i in range(1, size) if (i - 1 ^ 1) + 1 < size]

    def exchange(parts):
        return lax.ppermute(parts[0], "rows", inner), lax.ppermute(parts[1], "rows", outer)

    halo_a = exchange(pack(0, cut))
    packed_b = pack(cut, cols)
    halo_b = exchange(packed_b)

    prepare = pl.pallas_call(
        functools.partial(prepare_kernel, rows, inputs),
        out_shape=(
            shape(rows * inputs, cols),
            shape(5, tiles * rows, LANES),
            shape(tiles * rows, LANES),
        ),
        in_specs=[smem] + [vmem] * 6,
        out_specs=(vmem,) * 3,
        scratch_shapes=[pltpu.VMEM((rows * inputs, cols), F32)],
        compiler_params=params,
        cost_estimate=cost(10**9),
        name="prepare",
    )
    own, own_weights, scale = prepare(
        flag, field, streamwise, crossflow, diffusivity, obstacle, cell_weight
    )

    def march(first_pair, last_pair, sources, owned, halos):
        more = [shape(2, packed_rows, PAIR, dtype=BF16)] * (last_pair < pairs)
        chunk = (last_pair - first_pair) * PAIR
        return pl.pallas_call(
            functools.partial(
                march_kernel, rows, inputs, first_pair, last_pair, sources, owned, pairs
            ),
            out_shape=(
                shape(rows * inputs, chunk),
                *[shape(NSNAP * inputs, rows * chunk // 2, dtype=BF16)] * 2,
                *more,
            ),
            in_specs=[smem] + [vmem] * (3 + len(halos)),
            out_specs=(vmem,) * (3 + len(more)),
            scratch_shapes=[
                *[pltpu.VMEM(((span + 2) * inputs, chunk), F32)] * 2,
                pltpu.VMEM((coef_rows, chunk), F32),
                *[pltpu.VMEM((chunk // LANES * (span + 2 * SUB), LANES), F32)] * 5,
            ],
            compiler_params=params,
            cost_estimate=cost(10**9),
        )(flag, own, own_weights, scale, *halos)

    middle = LANES // 2
    last_a, kept_a, sent_a, both = march(
        0, shared + 1, [(0, p) for p in range(shared + 1)], (0, middle), halo_a
    )
    last_b, kept_b, sent_b = march(
        shared,
        pairs,
        [(0, 0)] + [(1, p) for p in range(pairs - shared - 1)],
        (middle, LANES),
        (both[0], both[1], *halo_b),
    )
    swap = [(0, 1), (1, 0)]
    other_a = lax.ppermute(sent_a, "fa", swap)
    other_b = lax.ppermute(sent_b, "fa", swap)
    total = pl.pallas_call(
        meet_kernel,
        out_shape=shape(NSNAP * inputs, NSNAP * inputs),
        in_specs=[smem] + [vmem] * 4,
        out_specs=vmem,
        compiler_params=params,
        name="meet",
    )(flag, kept_a, other_a, kept_b, other_b)
    total = total + lax.ppermute(total, "fa", swap)
    if size & (size - 1) == 0:
        stride = 1
        while stride < size:
            total = total + lax.ppermute(total, "rows", [(i, i ^ stride) for i in range(size)])
            stride *= 2
    else:
        total = lax.psum(total, "rows")
    hankel = total * (1.0 / math.sqrt(rows * size * cols))
    final = pl.pallas_call(
        functools.partial(finish_kernel, rows, inputs, shared),
        out_shape=shape(*field.shape),
        in_specs=[vmem] * 2,
        out_specs=vmem,
        compiler_params=params,
        cost_estimate=cost(10**7),
        name="finish",
    )(last_a, last_b)
    return (untiled(final, init_fields.shape[1:])[None], hankel)


def solution(mesh):
    placed = (
        P("fa", "ens", "rows", None),
        P("rows", None),
        P("rows", None),
        P("rows", None),
        P("rows", None),
        P("rows", None),
    )

    return jax.shard_map(
        local,
        mesh=mesh,
        in_specs=placed,
        out_specs=(P("fa", "ens", "rows", None), P("ens", None)),
        check_vma=False,
    )
```

```python
import functools
import math

import jax
import jax.numpy as jnp
from jax import lax
from jax.experimental import pallas as pl
from jax.experimental.pallas import tpu as pltpu
from jax.sharding import PartitionSpec as P


NSNAP = 4
STRIDE = 3
HALO = NSNAP * STRIDE
LANES = 128
SUB = 8
PAIR = 2 * LANES
F32 = jnp.float32
BF16 = jnp.bfloat16


def up8(count):
    return -(-count // SUB) * SUB


def lanes_of(tile):
    return slice(tile * LANES, (tile + 1) * LANES)


def tiled(array):
    inputs, rows, cols = array.shape
    split = array.reshape(inputs, rows // SUB, SUB, cols // LANES, LANES)
    return split.transpose(0, 1, 3, 2, 4).reshape(-1, LANES)


def untiled(array, shape):
    inputs, rows, cols = shape
    split = array.reshape(inputs, rows // SUB, cols // LANES, SUB, LANES)
    return split.transpose(0, 1, 3, 2, 4).reshape(shape)


def tile_of(rows, cols, row, tile, inputs):
    start = (row // SUB * (cols // LANES) + tile) * SUB + row % SUB
    return pl.ds(start, inputs, stride=rows * cols // LANES)


def sorting_matrix(back=False):
    source = lax.broadcasted_iota(jnp.int32, (PAIR, PAIR), 1 if back else 0)
    target = lax.broadcasted_iota(jnp.int32, (PAIR, PAIR), 0 if back else 1)
    wanted = jnp.where(target < LANES, 2 * target, 2 * (target - LANES) + 1)
    return jnp.where(source == wanted, 1.0, 0.0).astype(BF16)


def moved(part, matrix):
    return jnp.dot(part, matrix, preferred_element_type=F32)


def moved_whole(values, matrix):
    top = values.astype(BF16)
    rest = values - top.astype(F32)
    middle = rest.astype(BF16)
    bottom = (rest - middle.astype(F32)).astype(BF16)
    return (moved(top, matrix) + moved(middle, matrix)) + moved(bottom, matrix)


def eastern(tiles, tile, lane, count):
    if tile % 2 == 0:
        return tiles[tile + 1]
    after = tiles[(tile + 1) % count]
    return pltpu.roll(jnp.where(lane == 0, after, tiles[tile - 1]), LANES - 1, 1)


def western(tiles, tile, lane, count):
    if tile % 2 == 1:
        return tiles[tile - 1]
    before = tiles[(tile - 1) % count]
    return pltpu.roll(jnp.where(lane == LANES - 1, before, tiles[tile + 1]), 1, 1)


def weights_of(along, across, signed, is_adjoint, first_col=True, last_col=True):
    lane = lax.broadcasted_iota(jnp.int32, along[0].shape, 1)
    count = len(along)
    east, west, north, south, centre = [], [], [], [], []
    for tile in range(count):
        opened = jnp.where(signed[tile] < 0, 0.0, 1.0)
        spread = jnp.abs(signed[tile])
        half_x, half_y = along[tile] * 0.5, across[tile] * 0.5
        east.append(opened * (spread - half_x))
        west.append(opened * (spread + half_x))
        low, high = opened * (spread - half_y), opened * (spread + half_y)
        north.append(jnp.where(is_adjoint, high, low))
        south.append(jnp.where(is_adjoint, low, high))
        centre.append(opened * (1.0 - 4.0 * spread))
    east_w = [jnp.where(is_adjoint, eastern(west, t, lane, count), east[t]) for t in range(count)]
    west_w = [jnp.where(is_adjoint, western(east, t, lane, count), west[t]) for t in range(count)]
    if last_col:
        east_w[-1] = jnp.where(lane == LANES - 1, 0.0, east_w[-1])
    if first_col:
        west_w[0] = jnp.where(lane == 0, 0.0, west_w[0])
    return east_w, west_w, north, south, centre


def pack_kernel(
    rows, inputs, left, odd_ref, field_in, along_in, across_in, viscous_in, solid_in,
    inner, outer, coefs, field, along, across, viscous, solid, sems,
):
    cols = along.shape[1]
    right = left + inner.shape[1]
    copies = [
        pltpu.make_async_copy(source, target, sems.at[index])
        for index, (source, target) in enumerate(
            (
                (field_in, field),
                (along_in, along),
                (across_in, across),
                (viscous_in, viscous),
                (solid_in, solid),
            )
        )
    ]
    for copy in copies:
        copy.start()
    for copy in copies:
        copy.wait()
    is_odd = odd_ref[0] == 1
    signed = jnp.where(solid[:, left:right] != 0, -viscous[:, left:right], viscous[:, left:right])
    planes = (along[:, left:right], across[:, left:right], signed)

    def fill(out, first):
        for index, plane in enumerate(planes):
            coefs[index * HALO : (index + 1) * HALO, :] = plane[first : first + HALO]
        out[HALO * inputs :, :] = coefs[...].astype(out.dtype)
        for step in range(HALO):
            for tile in range(left // LANES, right // LANES):
                part = field[tile_of(rows, cols, first + step, tile, inputs), :]
                to = lanes_of(tile - left // LANES)
                out[step * inputs : (step + 1) * inputs, to] = part.astype(out.dtype)

    @pl.when(is_odd)
    def _():
        fill(inner, 0)
        fill(outer, rows - HALO)

    @pl.when(jnp.logical_not(is_odd))
    def _():
        fill(inner, rows - HALO)
        fill(outer, 0)


def prepare_kernel(
    rows, inputs, adjoint_ref, field, along, across, viscous, solid, area, own, weights, scale, lined
):
    is_adjoint = adjoint_ref[0] == 1
    cols = along.shape[1]
    matrix = sorting_matrix()
    for row in range(rows):
        for tile in range(cols // LANES):
            lined[row * inputs : (row + 1) * inputs, lanes_of(tile)] = field[
                tile_of(rows, cols, row, tile, inputs), :
            ]
    signed = jnp.where(solid[...] != 0, -viscous[...], viscous[...])
    factor = jnp.where(is_adjoint, area[...], 1.0)
    sorted_coefs = [[], [], []]
    for pair in range(cols // PAIR):
        at = slice(pair * PAIR, (pair + 1) * PAIR)
        own[:, at] = moved_whole(lined[:, at], matrix)
        for kept, values in zip(sorted_coefs, (along[:, at], across[:, at], signed[:, at])):
            values = moved_whole(values, matrix)
            kept += [values[:, :LANES], values[:, LANES:]]
        values = moved_whole(factor[:, at], matrix)
        for side in range(2):
            tile = 2 * pair + side
            scale[tile * rows : (tile + 1) * rows, :] = values[:, lanes_of(side)]
    for index, tiles in enumerate(weights_of(*sorted_coefs, is_adjoint)):
        for tile, values in enumerate(tiles):
            weights[index, tile * rows : (tile + 1) * rows, :] = values


def march_kernel(rows, inputs, first_pair, last_pair, sources, owned, all_pairs, adjoint_ref, odd_ref, own, own_weights, scale, *refs):
    count = 2 * (1 + max(operand for operand, _ in sources))
    halos, refs = refs[:count], refs[count:]
    both = None
    if last_pair < all_pairs:
        both = refs[3]
        refs = (*refs[:3], *refs[4:])
    last, kept, sent, state_a, state_b, coefs, east_w, west_w, north_w, south_w, centre_w = refs
    adjoint = adjoint_ref[0]
    is_adjoint = adjoint == 1
    is_odd = odd_ref[0] == 1
    tiles = 2 * (last_pair - first_pair)
    tile0 = 2 * first_pair
    span = rows + 2 * HALO
    wide = span + 2 * SUB
    matrix = sorting_matrix()
    all_weights = (east_w, west_w, north_w, south_w, centre_w)
    edges = (first_pair == 0, last_pair == all_pairs)

    def fill(low_at, high_at):
        for side, first, at_side in ((0, 0, low_at), (1, HALO + rows, high_at)):
            sorted_coefs = [[], [], []]
            for pair, (operand, place) in enumerate(sources):
                at = slice(pair * PAIR, (pair + 1) * PAIR)
                source = halos[2 * operand + at_side[operand]]
                source = source[:, place * PAIR : (place + 1) * PAIR]
                if both is not None and pair == len(sources) - 1:
                    both[side] = source
                values = moved(source, matrix)
                state_a[(1 + first) * inputs : (1 + first + HALO) * inputs, at] = values[
                    : HALO * inputs
                ]
                coefs[:, at] = values[HALO * inputs :]
                for index, taken in enumerate(sorted_coefs):
                    part = coefs[index * HALO : (index + 1) * HALO, at]
                    taken += [part[:, :LANES], part[:, LANES:]]
            for ref, values in zip(all_weights, weights_of(*sorted_coefs, is_adjoint, *edges)):
                for tile in range(tiles):
                    start = tile * wide + SUB + first
                    ref[start : start + HALO, :] = values[tile]

    fixed = (0,) * (len(halos) // 2 - 1), (1,) * (len(halos) // 2 - 1)

    @pl.when(is_odd)
    def _():
        fill((*fixed[0], 0), (*fixed[1], 1))

    @pl.when(jnp.logical_not(is_odd))
    def _():
        fill((*fixed[0], 1), (*fixed[1], 0))

    state_a[(1 + HALO) * inputs : (1 + HALO + rows) * inputs, :] = own[
        :, tile0 * LANES : (tile0 + tiles) * LANES
    ]
    for index, ref in enumerate(all_weights):
        for tile in range(tiles):
            start = tile * wide + SUB + HALO
            at = slice((tile0 + tile) * rows, (tile0 + tile + 1) * rows)
            ref[start : start + rows, :] = own_weights[index, at, :]

    states = (state_a, state_b)
    lane = lax.broadcasted_iota(jnp.int32, (inputs, LANES), 1)
    for step in range(1, HALO + 1):
        src, dst = states[(step - 1) % 2], states[step % 2]

        def line(row, src=src):
            at = slice((1 + row) * inputs, (2 + row) * inputs)
            return [src[at, lanes_of(tile)] for tile in range(tiles)]

        def weight(ref, row, tile):
            return ref[pl.ds(tile * wide + SUB + row, inputs, stride=0), :]

        behind, here = line(step - 1), line(step)
        for row in range(step, span - step):
            ahead = line(row + 1)
            for tile in range(tiles):
                total = weight(centre_w, row, tile) * here[tile]
                total += weight(north_w, row + adjoint, tile) * ahead[tile]
                total += weight(south_w, row - adjoint, tile) * behind[tile]
                total += weight(east_w, row, tile) * eastern(here, tile, lane, tiles)
                total += weight(west_w, row, tile) * western(here, tile, lane, tiles)
                dst[(1 + row) * inputs : (2 + row) * inputs, lanes_of(tile)] = total
            behind, here = here, ahead
        if step % STRIDE == 0:
            snap = slice((step // STRIDE - 1) * inputs, (step // STRIDE) * inputs)

            def record(first, second, scaled, dst=dst, snap=snap):
                for row in range(rows):
                    at = slice((1 + HALO + row) * inputs, (2 + HALO + row) * inputs)
                    for tile in range(tiles):
                        value = dst[at, lanes_of(tile)]
                        if scaled:
                            factor = pl.ds((tile0 + tile) * rows + row, inputs, stride=0)
                            value = value * scale[factor, :]
                        low_lane, high_lane = 0, LANES
                        if tile < 2:
                            low_lane = owned[0]
                        if tile >= tiles - 2:
                            high_lane = owned[1]
                        if low_lane > 0:
                            value = jnp.where(lane >= low_lane, value, 0.0)
                        if high_lane < LANES:
                            value = jnp.where(lane < high_lane, value, 0.0)
                        out = first if tile < tiles // 2 else second
                        start = (row * (tiles // 2) + tile % (tiles // 2)) * LANES
                        out[snap, start : start + LANES] = value.astype(out.dtype)

            @pl.when(is_adjoint)
            def _():
                record(sent, kept, True)

            @pl.when(jnp.logical_not(is_adjoint))
            def _():
                record(kept, sent, False)

    last[...] = states[HALO % 2][(1 + HALO) * inputs : (1 + HALO + rows) * inputs, :]


def meet_kernel(adjoint_ref, mine_a, other_a, mine_b, other_b, product):
    def met(rows, columns):
        return lax.dot_general(
            rows[...], columns[...], (((1,), (1,)), ((), ())), preferred_element_type=F32
        )

    @pl.when(adjoint_ref[0] == 0)
    def _():
        product[...] = met(other_a, mine_a) + met(other_b, mine_b)

    @pl.when(adjoint_ref[0] != 0)
    def _():
        product[...] = met(mine_a, other_a) + met(mine_b, other_b)


def finish_kernel(rows, inputs, shared, left, right, final):
    matrix = sorting_matrix(back=True)
    lane = lax.broadcasted_iota(jnp.int32, (rows * inputs, PAIR), 1)
    pairs = shared + right.shape[1] // PAIR
    for pair in range(pairs):
        if pair <= shared:
            values = left[:, pair * PAIR : (pair + 1) * PAIR]
        if pair >= shared:
            others = right[:, (pair - shared) * PAIR : (pair - shared + 1) * PAIR]
            values = jnp.where(lane % LANES < LANES // 2, values, others) if pair == shared else others
        values = moved_whole(values, matrix)
        for row in range(rows):
            for side in range(2):
                final[tile_of(rows, pairs * PAIR, row, 2 * pair + side, inputs), :] = values[
                    row * inputs : (row + 1) * inputs, lanes_of(side)
                ]


def local(init_fields, streamwise, crossflow, diffusivity, obstacle, cell_weight):
    adjoint = lax.axis_index("fa").astype(jnp.int32)
    flag = adjoint[None]
    odd = (lax.axis_index("rows").astype(jnp.int32) % 2)[None]
    _, inputs, rows, cols = init_fields.shape
    field = tiled(init_fields[0])
    coef_rows = up8(3 * HALO)
    packed_rows = HALO * inputs + coef_rows
    span = rows + 2 * HALO
    tiles = cols // LANES
    vmem = pl.BlockSpec(memory_space=pltpu.VMEM)
    smem = pl.BlockSpec(memory_space=pltpu.SMEM)

    def shape(*dims, dtype=F32):
        return jax.ShapeDtypeStruct(dims, dtype)

    def cost(amount):
        return pl.CostEstimate(flops=amount, bytes_accessed=4 * field.size * 4, transcendentals=0)

    params = pltpu.CompilerParams(vmem_limit_bytes=14 << 20)
    hbm = pl.BlockSpec(memory_space=pltpu.HBM)
    pairs = cols // PAIR
    shared = pairs // 2
    cut = (shared + 1) * PAIR
    plane = pltpu.VMEM((rows, cols), F32)
    grids = [
        pltpu.with_memory_space_constraint(x, pltpu.HBM)
        for x in (field, streamwise, crossflow, diffusivity, obstacle)
    ]

    def pack(left, right):
        return pl.pallas_call(
            functools.partial(pack_kernel, rows, inputs, left),
            out_shape=[shape(packed_rows, right - left, dtype=BF16)] * 2,
            in_specs=[smem] + [hbm] * 5,
            out_specs=[vmem] * 2,
            scratch_shapes=[
                pltpu.VMEM((coef_rows, right - left), F32),
                pltpu.VMEM(field.shape, F32),
                plane,
                plane,
                plane,
                pltpu.VMEM((rows, cols), jnp.int32),
                pltpu.SemaphoreType.DMA((5,)),
            ],
            compiler_params=params,
            cost_estimate=cost(10**8),
        )(odd, *grids)

    size = lax.axis_size("rows")
    inner = [(i, i ^ 1) for i in range(size) if i ^ 1 < size]
    outer = [(i, (i - 1 ^ 1) + 1) for i in range(1, size) if (i - 1 ^ 1) + 1 < size]

    def exchange(parts):
        return lax.ppermute(parts[0], "rows", inner), lax.ppermute(parts[1], "rows", outer)

    halo_a = exchange(pack(0, cut))
    packed_b = pack(cut, cols)
    halo_b = exchange(packed_b)

    prepare = pl.pallas_call(
        functools.partial(prepare_kernel, rows, inputs),
        out_shape=(
            shape(rows * inputs, cols),
            shape(5, tiles * rows, LANES),
            shape(tiles * rows, LANES),
        ),
        in_specs=[smem] + [vmem] * 6,
        out_specs=(vmem,) * 3,
        scratch_shapes=[pltpu.VMEM((rows * inputs, cols), F32)],
        compiler_params=params,
        cost_estimate=cost(10**9),
        name="prepare",
    )
    own, own_weights, scale = prepare(
        flag, field, streamwise, crossflow, diffusivity, obstacle, cell_weight
    )

    def march(first_pair, last_pair, sources, owned, halos):
        more = [shape(2, packed_rows, PAIR, dtype=BF16)] * (last_pair < pairs)
        chunk = (last_pair - first_pair) * PAIR
        return pl.pallas_call(
            functools.partial(
                march_kernel, rows, inputs, first_pair, last_pair, sources, owned, pairs
            ),
            out_shape=(
                shape(rows * inputs, chunk),
                *[shape(NSNAP * inputs, rows * chunk // 2, dtype=BF16)] * 2,
                *more,
            ),
            in_specs=[smem] * 2 + [vmem] * (3 + len(halos)),
            out_specs=(vmem,) * (3 + len(more)),
            scratch_shapes=[
                *[pltpu.VMEM(((span + 2) * inputs, chunk), F32)] * 2,
                pltpu.VMEM((coef_rows, chunk), F32),
                *[pltpu.VMEM((chunk // LANES * (span + 2 * SUB), LANES), F32)] * 5,
            ],
            compiler_params=params,
            cost_estimate=cost(10**9),
        )(flag, odd, own, own_weights, scale, *halos)

    middle = LANES // 2
    last_a, kept_a, sent_a, both = march(
        0, shared + 1, [(0, p) for p in range(shared + 1)], (0, middle), halo_a
    )
    last_b, kept_b, sent_b = march(
        shared,
        pairs,
        [(0, 0)] + [(1, p) for p in range(pairs - shared - 1)],
        (middle, LANES),
        (both[0], both[1], *halo_b),
    )
    swap = [(0, 1), (1, 0)]
    other_a = lax.ppermute(sent_a, "fa", swap)
    other_b = lax.ppermute(sent_b, "fa", swap)
    total = pl.pallas_call(
        meet_kernel,
        out_shape=shape(NSNAP * inputs, NSNAP * inputs),
        in_specs=[smem] + [vmem] * 4,
        out_specs=vmem,
        compiler_params=params,
        name="meet",
    )(flag, kept_a, other_a, kept_b, other_b)
    total = total + lax.ppermute(total, "fa", swap)
    if size & (size - 1) == 0:
        stride = 1
        while stride < size:
            total = total + lax.ppermute(total, "rows", [(i, i ^ stride) for i in range(size)])
            stride *= 2
    else:
        total = lax.psum(total, "rows")
    hankel = total * (1.0 / math.sqrt(rows * size * cols))
    final = pl.pallas_call(
        functools.partial(finish_kernel, rows, inputs, shared),
        out_shape=shape(*field.shape),
        in_specs=[vmem] * 2,
        out_specs=vmem,
        compiler_params=params,
        cost_estimate=cost(10**7),
        name="finish",
    )(last_a, last_b)
    return (untiled(final, init_fields.shape[1:])[None], hankel)


def solution(mesh):
    placed = (
        P("fa", "ens", "rows", None),
        P("rows", None),
        P("rows", None),
        P("rows", None),
        P("rows", None),
        P("rows", None),
    )

    return jax.shard_map(
        local,
        mesh=mesh,
        in_specs=placed,
        out_specs=(P("fa", "ens", "rows", None), P("ens", None)),
        check_vma=False,
    )
```
